128 devices in a mesh: grp: 16 (over z, y_hi, core), brk: 8 (over y_lo, x).
Axes of the slice: x: 4, y: 4 (y_hi: 2, y_lo: 2; y = y_hi * 2 + y_lo), z: 4, core: 2. Of those that a mesh axis runs over, the one named last changes fastest.
Arguments:
- state: float32 [16, 5, 384, 64, 128], P('grp', None, 'brk'), may hold values from -6 to 6
- adjoint: float32 [16, 5, 384, 64, 128], P('grp', None, 'brk'), may hold values from -6 to 6
- source: float32 [16, 5, 384, 64, 128], P('grp', None, 'brk'), may hold values from -6 to 6
- kappa: float32 [16, 384, 64, 128], P('grp', 'brk'), may hold values from 0.2 to 3
- cut_flags: int32 [16, 384, 64, 128], P('grp', 'brk'), may hold values 0 or 1
- coupling: float32 [5, 5], replicated, may hold values from -2.5 to 2.5
- target: int32 [128, 128], replicated, may hold values from 0 to 16383, as said below
Outputs:
- estimate: float32 [16384, 5, 384], P(('grp', 'brk'))
The draws below stay inside these ranges and needn't reach their ends.
Inputs may be any that keep to these rules, and one draw needn't show every extreme that they name: `target`: each value owner * 128 + slot appears exactly once; the owner is never in the sender's own level group; a brick sends at most 2 tiles to one owner, and exactly 2 to some owners.
All inputs are finite; a program needn't handle non-finite values. No bound on the sum of `cut_flags` on one device may be relied on, other than what follows from the above.
Results may differ from the reference program's by a relative error of at most 0.00007.
Values sent between devices are 32-bit elements; how exact they have to be, the bound alone decides.
No kernel may reach another device: no remote copies, remote signals or barrier semaphores. Data moves between devices by JAX's collectives and lax.ppermute only.
A program may use at most 512 MiB of HBM per device.

```python
import math
import jax
import jax.numpy as jnp
from jax import lax

FIELDS = 5
BY = 64
BZ = 128
TPD = 128
NGROUP = 16
NBRICK = 8
OWNERS = 128
NX = 384
TILE = 384


def draw_target(key, part):
    pair_count = (NGROUP - 1) * NBRICK
    owner_count = NGROUP * NBRICK
    key_pairs, key_tiles, key_slots = jax.random.split(key, 3)
    cycled = jnp.arange(TPD, dtype=jnp.int32) % pair_count
    relabel = jax.random.permutation(key_pairs, pair_count).astype(jnp.int32)
    shift_id = relabel[cycled]
    shift_grp = 1 + shift_id // NBRICK
    shift_brk = shift_id % NBRICK
    devices = jnp.arange(owner_count, dtype=jnp.int32)
    group_of = devices // NBRICK
    brick_of = devices % NBRICK
    tile_keys = jax.random.split(key_tiles, owner_count)
    ordering = jax.vmap(lambda subkey: jax.random.permutation(subkey, TPD))(tile_keys).astype(jnp.int32)
    owner_grp = (group_of[:, None] + shift_grp[ordering]) % NGROUP
    owner_brk = (brick_of[:, None] + shift_brk[ordering]) % NBRICK
    owner_id = owner_grp * NBRICK + owner_brk
    slot_keys = jax.random.split(key_slots, owner_count)
    slotting = jax.vmap(lambda subkey: jax.random.permutation(subkey, TPD))(slot_keys).astype(jnp.int32)
    slot_id = slotting[owner_id, ordering]
    return (owner_id * TPD + slot_id).astype(jnp.int32)


def place_ends(entries, own_key, least, largest):
    longest = entries.shape.index(max(entries.shape))
    spots = []
    for shift in (0, 1):
        where = [jax.random.randint(jax.random.fold_in(own_key, axis), (), 0, length) for axis, length in enumerate(entries.shape)]
        where[longest] = (where[longest] + shift) % entries.shape[longest]
        spots.append(tuple(where))
    return entries.at[spots[0]].set(least).at[spots[1]].set(largest)


def shard_levels(rng, extent, cuts, low, largest):
    factor_of = 1.0
    for position, parts in cuts:
        draws = jax.random.uniform(jax.random.fold_in(jax.random.fold_in(rng, 6), position), (parts,), jnp.float32, low / len(cuts), largest / len(cuts))
        factor_of = factor_of * jnp.repeat(jnp.exp(draws), extent[position] // parts).reshape((-1,) + (1,) * (len(extent) - 1 - position))
    return factor_of


def gaussian(own_key, extent, width, bound, cuts=(), held_as=jnp.bfloat16):
    values = jax.random.normal(own_key, extent, jnp.float32) * width
    if len(cuts) > 0:
        values = shard_levels(own_key, extent, cuts, -0.22, 0.18) * values
    return jnp.clip(values, min=-bound, max=bound).astype(held_as)


def setup_inputs(seed: int = 0) -> dict:
    key_of = jax.random.split(jax.random.key(seed), 8)
    state = gaussian(key_of[0], (NGROUP, FIELDS, NX, BY, BZ), 1.0, 6.0, ((0, 16), (2, 8)), jnp.float32)
    adjoint = gaussian(key_of[1], (NGROUP, FIELDS, NX, BY, BZ), 1.0, 6.0, ((0, 16), (2, 8)), jnp.float32)
    source = gaussian(key_of[2], (NGROUP, FIELDS, NX, BY, BZ), 1.0, 6.0, ((0, 16), (2, 8)), jnp.float32)
    kappa = jnp.clip(jnp.exp(math.log(3.0) - 2.7080502 * jax.random.uniform(key_of[3], (NGROUP, NX, BY, BZ), jnp.float32) ** shard_levels(key_of[3], (NGROUP, NX, BY, BZ), ((0, 16), (1, 8)), -0.2, 0.2)), 0.2, 3.0)
    cut_flags = place_ends((jax.random.randint(key_of[4], (NGROUP, NX, BY, BZ), 0, 3) < 1).astype(jnp.int32), jax.random.fold_in(key_of[4], 1), 0, 1)
    coupling = gaussian(key_of[5], (FIELDS, FIELDS), FIELDS ** -0.5, 2.5, (), jnp.float32)
    target = draw_target(jax.random.fold_in(key_of[7], 71), 0)
    return {"state": state, "adjoint": adjoint, "source": source, "kappa": kappa, "cut_flags": cut_flags, "coupling": coupling, "target": target}


def stencil_apply(values, kappa_cells, coupling):
    padded = jnp.pad(values, ((0, 0), (1, 1), (1, 1), (1, 1)))
    neighbours = padded[:, 2:, 1:-1, 1:-1] + padded[:, :-2, 1:-1, 1:-1]
    neighbours = neighbours + padded[:, 1:-1, 2:, 1:-1] + padded[:, 1:-1, :-2, 1:-1]
    neighbours = neighbours + padded[:, 1:-1, 1:-1, 2:] + padded[:, 1:-1, 1:-1, :-2]
    coupled = jnp.einsum("fg,gxyz->fxyz", coupling.astype(jnp.float32), values.astype(jnp.float32), precision=lax.Precision.HIGHEST)
    return (6.0 + kappa_cells[None]) * values - neighbours + coupled


def reference(state, adjoint, source, kappa, cut_flags, coupling, target):
    fields = state.shape[1]
    cells_x = state.shape[2]
    cells_y = state.shape[3]
    cells_z = state.shape[4]

    def one_group(inputs):
        values, dual, rhs, kappa_cells, flags = inputs
        residual = rhs - stencil_apply(values, kappa_cells, coupling)
        weighted = (1.0 - 0.5 * flags.astype(jnp.float32))[None] * dual * residual
        coarse = weighted.reshape(fields, cells_x // 2, 2, cells_y // 2, 2, cells_z // 2, 2).sum(axis=(2, 4, 6))
        coarse = coarse.reshape(fields, NBRICK, TPD, TILE)
        return coarse.transpose(1, 2, 0, 3)

    pieces = lax.map(one_group, (state, adjoint, source, kappa, cut_flags))
    pieces = pieces.reshape(-1, fields, TILE)
    estimate = jnp.zeros((OWNERS * TPD, fields, TILE), jnp.float32)
    return estimate.at[target.reshape(-1)].set(pieces)
```

```python
import functools
import jax
import jax.numpy as jnp
from jax import lax
from jax.experimental import pallas as pl
from jax.experimental.pallas import tpu as pltpu
from jax.sharding import PartitionSpec as P

VMEM_LIMIT = 56 * 1024 * 1024
AHEAD = 5


def weight_of(flags):
    return 1.0 - 0.5 * flags.astype(jnp.float32)


def pool_matrix(lanes):
    row = lax.broadcasted_iota(jnp.int32, (2 * lanes, lanes), 0)
    col = lax.broadcasted_iota(jnp.int32, (2 * lanes, lanes), 1)
    return jnp.where(row // 2 == col, 1.0, 0.0).astype(jnp.bfloat16)


def pooled_rows(fine_ref, fields, cells_y, matrix):
    rows = cells_y // 4
    parts = [[fine_ref[f, pl.ds(k, rows, stride=4), :] for k in range(4)] for f in range(fields)]
    low = jnp.concatenate([p[0] + p[1] for p in parts], axis=0)
    high = jnp.concatenate([p[2] + p[3] for p in parts], axis=0)
    both = jnp.concatenate([low, high], axis=1)
    first = both.astype(jnp.bfloat16)
    rest = both - first.astype(jnp.float32)
    second = rest.astype(jnp.bfloat16)
    dot = functools.partial(jnp.dot, preferred_element_type=jnp.float32)
    return dot(first, matrix) + dot(second, matrix)


def main_kernel(state, adjoint, source, kappa, flags, coupling, out, sv, av, bv, kv, fv, wv, pv, sems):
    fields, cells_x, cells_y, lanes = adjoint.shape
    steps = cells_x // 2
    rows = cells_y // 4

    def copy(step, i):
        at = pl.ds(2 * step, 2)
        if i == 0:
            landing = sv.at[:, pl.ds(2 * step + 1, 2), pl.ds(8, cells_y)]
            return pltpu.make_async_copy(state.at[:, at], landing, sems.at[step, 0])
        if i < 3:
            src, dst = ((adjoint, av), (source, bv))[i - 1]
            return pltpu.make_async_copy(src.at[:, at], dst.at[:, at], sems.at[step, i])
        src, dst = ((kappa, kv), (flags, fv))[i - 3]
        return pltpu.make_async_copy(src.at[at], dst.at[at], sems.at[step, i])

    def start(step):
        for i in range(5):
            copy(step, i).start()

    for step in range(AHEAD):
        start(step)
    zero = jnp.zeros((8, lanes), jnp.float32)
    pv[...] = pool_matrix(lanes)

    def clear(x, carry):
        for f in range(fields):
            sv[f, x, pl.ds(0, 8), :] = zero
            sv[f, x, pl.ds(cells_y + 8, 8), :] = zero
        return carry

    lax.fori_loop(0, cells_x + 2, clear, 0)
    for f in range(fields):
        for y in range(0, cells_y, 8):
            sv[f, 0, pl.ds(y + 8, 8), :] = zero
            sv[f, cells_x + 1, pl.ds(y + 8, 8), :] = zero

    coef = [[coupling[f, h] for h in range(fields)] for f in range(fields)]
    lane = lax.broadcasted_iota(jnp.int32, (8, lanes), 1)
    inner_lo = lane != 0
    inner_hi = lane != lanes - 1
    copy(0, 0).wait()

    def step_body(step, carry):
        @pl.when(step + AHEAD < steps)
        def _():
            start(step + AHEAD)

        @pl.when(step + 1 < steps)
        def _():
            copy(step + 1, 0).wait()

        for i in range(1, 5):
            copy(step, i).wait()

        for y in range(0, cells_y, 8):
            total = [None] * fields
            for p in range(2):
                x = 2 * step + p
                kap = kv[x, pl.ds(y, 8), :]
                wgt = weight_of(fv[x, pl.ds(y, 8), :])
                mid = [sv[f, x + 1, pl.ds(y + 8, 8), :] for f in range(fields)]
                for f in range(fields):
                    near = sv[f, x, pl.ds(y + 8, 8), :] + sv[f, x + 2, pl.ds(y + 8, 8), :]
                    near = near + sv[f, x + 1, pl.ds(y + 7, 8), :] + sv[f, x + 1, pl.ds(y + 9, 8), :]
                    near = near + jnp.where(inner_lo, pltpu.roll(mid[f], 1, 1), 0.0)
                    near = near + jnp.where(inner_hi, pltpu.roll(mid[f], lanes - 1, 1), 0.0)
                    applied = (kap + (coef[f][f] + 6.0)) * mid[f]
                    for h in range(fields):
                        if h != f:
                            applied = applied + coef[f][h] * mid[h]
                    residual = bv[f, x, pl.ds(y, 8), :] - applied + near
                    term = wgt * av[f, x, pl.ds(y, 8), :] * residual
                    total[f] = term if p == 0 else total[f] + term
            for f in range(fields):
                wv[f, pl.ds(y, 8), :] = total[f]
        pooled = pooled_rows(wv, fields, cells_y, pv[...])
        for f in range(fields):
            out[f, pl.ds(pl.multiple_of(step * rows, rows), rows), :] = pooled[f * rows : (f + 1) * rows]
        return carry

    lax.fori_loop(0, steps, step_body, 0)


def main_part(state, adjoint, source, kappa, flags, coupling):
    fields, cells_x, cells_y, lanes = state.shape
    f32 = jnp.float32
    anyspace = pl.BlockSpec(memory_space=pl.ANY)
    return pl.pallas_call(
        main_kernel,
        out_shape=jax.ShapeDtypeStruct((fields, cells_x * cells_y // 8, lanes), f32),
        in_specs=[anyspace] * 5 + [pl.BlockSpec(memory_space=pltpu.SMEM)],
        out_specs=pl.BlockSpec(memory_space=pltpu.VMEM),
        scratch_shapes=[
            pltpu.VMEM((fields, cells_x + 2, cells_y + 16, lanes), f32),
            pltpu.VMEM((fields, cells_x, cells_y, lanes), f32),
            pltpu.VMEM((fields, cells_x, cells_y, lanes), f32),
            pltpu.VMEM((cells_x, cells_y, lanes), f32),
            pltpu.VMEM((cells_x, cells_y, lanes), jnp.int32),
            pltpu.VMEM((fields, cells_y, lanes), f32),
            pltpu.VMEM((2 * lanes, lanes), jnp.bfloat16),
            pltpu.SemaphoreType.DMA((cells_x // 2, 5)),
        ],
        compiler_params=pltpu.CompilerParams(vmem_limit_bytes=VMEM_LIMIT),
        cost_estimate=pl.CostEstimate(flops=100_000_000, bytes_accessed=27_700_000, transcendentals=0),
        name="residual_pool",
    )(state, adjoint, source, kappa, flags, coupling)


def pack_kernel(capacity, tiles, part, before, after, adj_lo, adj_hi, flag_lo, flag_hi, out, wv, pv, slots, seen):
    fields, cells_y, lanes = before.shape
    rows = cells_y // 4
    per_dev = tiles.shape[1]
    cells = part.shape[1]
    span = cells // per_dev

    def clear(i, carry):
        seen[i] = 0
        return carry

    lax.fori_loop(0, per_dev, clear, 0)

    def rank(t, carry):
        owner = lax.shift_right_logical(tiles[0, t], per_dev.bit_length() - 1)
        count = seen[owner]
        slots[t] = (owner * capacity + count) * (span * fields)
        seen[owner] = count + 1
        return carry

    lax.fori_loop(0, per_dev, rank, 0)
    pv[...] = pool_matrix(lanes)
    for face, dual, flag, at in ((before, adj_lo, flag_lo, 0), (after, adj_hi, flag_hi, cells - rows)):
        for y in range(0, cells_y, 8):
            wgt = weight_of(flag[0, pl.ds(y, 8), :])
            for f in range(fields):
                wv[f, pl.ds(y, 8), :] = wgt * dual[f, 0, pl.ds(y, 8), :] * face[f, pl.ds(y, 8), :]
        pooled = pooled_rows(wv, fields, cells_y, pv[...])
        for f in range(fields):
            part[f, pl.ds(at, rows), :] = part[f, pl.ds(at, rows), :] + pooled[f * rows : (f + 1) * rows]

    def place(t, carry):
        base = slots[t]
        for f in range(fields):
            for j in range(span):
                out[pl.ds(base + f * span + j, 1), :] = part[f, pl.ds(t * span + j, 1), :]
        return carry

    lax.fori_loop(0, per_dev, place, 0)


def pack_part(part, before, after, adjoint, flags, tiles, capacity, owners):
    fields, cells_x, cells_y, lanes = adjoint.shape
    per_dev = tiles.shape[1]
    span = part.shape[1] // per_dev
    f32 = jnp.float32

    def plane(x):
        return pl.BlockSpec((fields, 1, cells_y, lanes), lambda i: (0, x, 0, 0))

    def flag_plane(x):
        return pl.BlockSpec((1, cells_y, lanes), lambda i: (x, 0, 0))

    def whole(a):
        return pl.BlockSpec(a.shape, lambda i: (0,) * a.ndim)

    def body(tiles, part_in, *refs):
        part_ref = refs[-1]
        part_ref[...] = part_in[...]
        pack_kernel(capacity, tiles, part_ref, *refs[:-1])

    n_rows = owners * capacity * span * fields
    return pl.pallas_call(
        body,
        grid=(1,),
        out_shape=jax.ShapeDtypeStruct((n_rows, lanes), f32),
        in_specs=[
            pl.BlockSpec(memory_space=pltpu.SMEM),
            whole(part),
            whole(before),
            whole(after),
            plane(0),
            plane(cells_x - 1),
            flag_plane(0),
            flag_plane(cells_x - 1),
        ],
        out_specs=pl.BlockSpec((n_rows, lanes), lambda i: (0, 0)),
        scratch_shapes=[
            pltpu.VMEM((fields, cells_y, lanes), f32),
            pltpu.VMEM((2 * lanes, lanes), jnp.bfloat16),
            pltpu.SMEM((per_dev,), jnp.int32),
            pltpu.SMEM((owners,), jnp.int32),
            pltpu.VMEM(part.shape, f32),
        ],
        compiler_params=pltpu.CompilerParams(vmem_limit_bytes=VMEM_LIMIT),
        cost_estimate=pl.CostEstimate(flops=1_000_000, bytes_accessed=3_500_000, transcendentals=0),
        name="edges_pack",
    )(tiles, part, before, after, adjoint, adjoint, flags, flags)


def unpack_kernel(lookup, received, out):
    fields, per_dev, width = out.shape
    lanes = received.shape[1]
    span = width // lanes

    sub = lax.broadcasted_iota(jnp.int32, (8, lanes), 0)

    def place(g, carry):
        bases = [lookup[g * 8 + s] * (span * fields) for s in range(8)]
        for f in range(fields):
            for j in range(span):
                rows = [received[pl.ds(b + f * span + j, 8, stride=0), :] for b in bases]
                value = rows[0]
                for s in range(1, 8):
                    value = jnp.where(sub == s, rows[s], value)
                out[f, pl.ds(pl.multiple_of(g * 8, 8), 8), pl.ds(j * lanes, lanes)] = value
        return carry

    lax.fori_loop(0, per_dev // 8, place, 0)


def unpack_part(lookup, received, fields, per_dev, width):
    vmem = pl.BlockSpec(memory_space=pltpu.VMEM)
    return pl.pallas_call(
        unpack_kernel,
        out_shape=jax.ShapeDtypeStruct((fields, per_dev, width), jnp.float32),
        in_specs=[pl.BlockSpec(memory_space=pltpu.SMEM), vmem],
        out_specs=vmem,
        compiler_params=pltpu.CompilerParams(vmem_limit_bytes=VMEM_LIMIT),
        cost_estimate=pl.CostEstimate(flops=0, bytes_accessed=3_000_000, transcendentals=0),
        name="unpack",
    )(lookup, received)


def local(state, adjoint, source, kappa, cut_flags, coupling, target):
    state, adjoint, source, kappa, flags = (a[0] for a in (state, adjoint, source, kappa, cut_flags))
    fields, cells_x, cells_y, lanes = state.shape
    groups, bricks = lax.axis_size("grp"), lax.axis_size("brk")
    owners = groups * bricks
    per_dev = target.shape[1]
    capacity = per_dev // ((groups - 1) * bricks) + 1
    width = cells_x * cells_y * lanes // 8 // per_dev
    myself = lax.axis_index(("grp", "brk"))

    up = [(i, i + 1) for i in range(bricks - 1)]
    down = [(j, i) for i, j in up]
    before = lax.ppermute(state[:, cells_x - 1], "brk", up)
    after = lax.ppermute(state[:, 0], "brk", down)

    part = main_part(state, adjoint, source, kappa, flags, coupling)
    mine = lax.dynamic_slice_in_dim(target, myself, 1, 0)
    outgoing = pack_part(part, before, after, adjoint, flags, mine, capacity, owners)
    incoming = lax.all_to_all(outgoing, ("grp", "brk"), 0, 0, tiled=True)

    slot_ids = myself * per_dev + jnp.arange(per_dev, dtype=jnp.int32)
    codes = jnp.arange(owners * per_dev, dtype=jnp.int32)
    hit = target.reshape(-1)[None, :] == slot_ids[:, None]
    origin = jnp.sum(jnp.where(hit, codes[None, :], 0), axis=1)
    sender = origin // per_dev
    before_it = jnp.logical_and(sender[:, None] == sender[None, :], origin[None, :] < origin[:, None])
    lookup = sender * capacity + jnp.sum(before_it.astype(jnp.int32), axis=1)
    out = unpack_part(lookup, incoming, fields, per_dev, width)
    return out.transpose(1, 0, 2)


def solution(mesh):
    placed = (
        P("grp", None, "brk", None, None),
        P("grp", None, "brk", None, None),
        P("grp", None, "brk", None, None),
        P("grp", "brk", None, None),
        P("grp", "brk", None, None),
        P(),
        P(),
    )
    return jax.shard_map(
        local, mesh=mesh, in_specs=placed, out_specs=P(("grp", "brk"), None, None), check_vma=False
    )
```

```python
import functools
import jax
import jax.numpy as jnp
from jax import lax
from jax.experimental import pallas as pl
from jax.experimental.pallas import tpu as pltpu
from jax.sharding import PartitionSpec as P

MIB = 1024 * 1024
PLANES = 4
AHEAD = 6
PAD = 8


def in_hbm(x):
    return pltpu.with_memory_space_constraint(x, pltpu.HBM)


def weight_of(flags):
    return 1.0 - 0.5 * flags.astype(jnp.float32)


def pool_matrix(lanes):
    row = lax.broadcasted_iota(jnp.int32, (2 * lanes, lanes), 0)
    col = lax.broadcasted_iota(jnp.int32, (2 * lanes, lanes), 1)
    return jnp.where(row // 2 == col, 1.0, 0.0).astype(jnp.bfloat16)


def pooled_rows(fine_ref, matrix):
    fields, cells_y, _ = fine_ref.shape
    rows = cells_y // 4
    parts = [[fine_ref[f, pl.ds(k, rows, stride=4), :] for k in range(4)] for f in range(fields)]
    low = jnp.concatenate([p[0] + p[1] for p in parts], axis=0)
    high = jnp.concatenate([p[2] + p[3] for p in parts], axis=0)
    both = jnp.concatenate([low, high], axis=1)
    first = both.astype(jnp.bfloat16)
    rest = both - first.astype(jnp.float32)
    second = rest.astype(jnp.bfloat16)
    dot = functools.partial(jnp.dot, preferred_element_type=jnp.float32)
    return dot(first, matrix) + dot(second, matrix)


def face_kernel(state, first, last, sems):
    cells_x = state.shape[1]
    one = pltpu.make_async_copy(state.at[:, 0], first, sems.at[0])
    two = pltpu.make_async_copy(state.at[:, cells_x - 1], last, sems.at[1])
    one.start()
    two.start()
    one.wait()
    two.wait()


def faces_of(state):
    fields, _, cells_y, lanes = state.shape
    face = jax.ShapeDtypeStruct((fields, cells_y, lanes), jnp.float32)
    vmem = pl.BlockSpec(memory_space=pltpu.VMEM)
    return pl.pallas_call(
        face_kernel,
        out_shape=(face, face),
        in_specs=[pl.BlockSpec(memory_space=pltpu.HBM)],
        out_specs=(vmem, vmem),
        scratch_shapes=[pltpu.SemaphoreType.DMA((2,))],
        compiler_params=pltpu.CompilerParams(vmem_limit_bytes=2 * MIB),
        cost_estimate=pl.CostEstimate(flops=0, bytes_accessed=650_000, transcendentals=0),
        name="faces",
    )(in_hbm(state))


def main_kernel(
    capacity, span, myself, coupling, target, state, adjoint, source, kv, fv,
    out, slots, sv, av, bv, wv, pv, tv, seen, sems, tsem,
):
    fields, cells_x, cells_y, lanes = adjoint.shape
    steps = cells_x // PLANES
    rows = cells_y // 4
    owners, per_dev = target.shape

    def copy(step, i):
        at = pl.ds(PLANES * step, PLANES)
        if i == 0:
            landing = sv.at[:, pl.ds(PLANES * step + 1, PLANES), pl.ds(8, cells_y)]
            return pltpu.make_async_copy(state.at[:, at], landing, sems.at[step, 0])
        src, dst = ((adjoint, av), (source, bv))[i - 1]
        return pltpu.make_async_copy(src.at[:, at], dst.at[:, at], sems.at[step, i])

    def start(step):
        for i in range(3):
            copy(step, i).start()

    me = myself[0]
    row8 = pl.multiple_of(lax.shift_left(lax.shift_right_logical(me, 3), 3), 8)
    table = pltpu.make_async_copy(target.at[pl.ds(row8, 8)], tv, tsem.at[0])
    table.start()
    for step in range(AHEAD):
        start(step)
    zero = jnp.zeros((8, lanes), jnp.float32)
    pv[...] = pool_matrix(lanes)

    def clear(x, carry):
        for f in range(fields):
            sv[f, x, pl.ds(0, 8), :] = zero
            sv[f, x, pl.ds(cells_y + 8, 8), :] = zero
        return carry

    lax.fori_loop(0, cells_x + 2, clear, 0)
    for f in range(fields):
        for y in range(0, cells_y, 8):
            sv[f, 0, pl.ds(y + 8, 8), :] = zero
            sv[f, cells_x + 1, pl.ds(y + 8, 8), :] = zero

    for i in range(owners):
        seen[i] = 0
    table.wait()
    mine = lax.bitwise_and(me, 7)

    def rank(t, carry):
        owner = lax.shift_right_logical(tv[mine, t], per_dev.bit_length() - 1)
        count = seen[owner]
        slots[t] = owner * capacity + count
        seen[owner] = count + 1
        return carry

    lax.fori_loop(0, per_dev, rank, 0, unroll=8)

    coef = [[coupling[f, h] for h in range(fields)] for f in range(fields)]
    lane = lax.broadcasted_iota(jnp.int32, (8, lanes), 1)
    inner_lo = lane != 0
    inner_hi = lane != lanes - 1

    def pool(half, at):
        pooled = pooled_rows(wv.at[half], pv[...])
        for f in range(fields):
            out[f, pl.ds(pl.multiple_of(at + PAD, 8), rows), :] = pooled[f * rows : (f + 1) * rows]

    copy(0, 0).wait()

    def step_body(step, carry):
        @pl.when(step + AHEAD < steps)
        def _():
            start(step + AHEAD)

        @pl.when(step + 1 < steps)
        def _():
            copy(step + 1, 0).wait()

        copy(step, 1).wait()
        copy(step, 2).wait()

        for half in range(PLANES // 2):
            coarse = step * (PLANES // 2) + half
            pool(1 - half % 2, jnp.maximum(coarse - 1, 0) * rows)
            for y in range(0, cells_y, 8):
                total = [None] * fields
                for p in range(2):
                    x = 2 * coarse + p
                    kap = kv[x, pl.ds(y, 8), :]
                    wgt = weight_of(fv[x, pl.ds(y, 8), :])
                    mid = [sv[f, x + 1, pl.ds(y + 8, 8), :] for f in range(fields)]
                    for f in range(fields):
                        near = sv[f, x, pl.ds(y + 8, 8), :] + sv[f, x + 2, pl.ds(y + 8, 8), :]
                        near = near + sv[f, x + 1, pl.ds(y + 7, 8), :] + sv[f, x + 1, pl.ds(y + 9, 8), :]
                        near = near + jnp.where(inner_lo, pltpu.roll(mid[f], 1, 1), 0.0)
                        near = near + jnp.where(inner_hi, pltpu.roll(mid[f], lanes - 1, 1), 0.0)
                        applied = (kap + (coef[f][f] + 6.0)) * mid[f]
                        for h in range(fields):
                            if h != f:
                                applied = applied + coef[f][h] * mid[h]
                        residual = bv[f, x, pl.ds(y, 8), :] - applied + near
                        term = wgt * av[f, x, pl.ds(y, 8), :] * residual
                        total[f] = term if p == 0 else total[f] + term
                for f in range(fields):
                    wv[half % 2, f, pl.ds(y, 8), :] = total[f]
        return carry

    lax.fori_loop(0, steps, step_body, 0)
    pool(1, (cells_x // 2 - 1) * rows)


def main_part(state, adjoint, source, kappa, flags, coupling, target, myself, capacity, span):
    fields, cells_x, cells_y, lanes = state.shape
    owners, per_dev = target.shape
    f32 = jnp.float32
    hbm = pl.BlockSpec(memory_space=pltpu.HBM)
    vmem = pl.BlockSpec(memory_space=pltpu.VMEM)
    smem = pl.BlockSpec(memory_space=pltpu.SMEM)
    return pl.pallas_call(
        functools.partial(main_kernel, capacity, span),
        out_shape=(
            jax.ShapeDtypeStruct((fields, cells_x * cells_y // 8 + 2 * PAD, lanes), f32),
            jax.ShapeDtypeStruct((per_dev,), jnp.int32),
        ),
        in_specs=[smem, smem, hbm, hbm, hbm, hbm, vmem, vmem],
        out_specs=(vmem, smem),
        scratch_shapes=[
            pltpu.VMEM((fields, cells_x + 2, cells_y + 16, lanes), f32),
            pltpu.VMEM((fields, cells_x, cells_y, lanes), f32),
            pltpu.VMEM((fields, cells_x, cells_y, lanes), f32),
            pltpu.VMEM((2, fields, cells_y, lanes), f32),
            pltpu.VMEM((2 * lanes, lanes), jnp.bfloat16),
            pltpu.SMEM((8, per_dev), jnp.int32),
            pltpu.SMEM((owners,), jnp.int32),
            pltpu.SemaphoreType.DMA((cells_x // PLANES, 3)),
            pltpu.SemaphoreType.DMA((1,)),
        ],
        compiler_params=pltpu.CompilerParams(vmem_limit_bytes=36 * MIB),
        cost_estimate=pl.CostEstimate(flops=100_000_000, bytes_accessed=27_700_000, transcendentals=0),
        name="residual_pool",
    )(myself, coupling, target, in_hbm(state), in_hbm(adjoint), in_hbm(source), kappa, flags)


def pack_kernel(tile_rows, slots, part, before, after, adjoint, flags, out, stage, pp, wv, pv, ev, gv, sems, tsem):
    fields, cells_y, lanes = before.shape
    cells_x = adjoint.shape[1]
    rows = cells_y // 4
    per_dev = slots.shape[0]
    cells = part.shape[1] - 2 * PAD
    span = cells // per_dev
    copies = []
    for i, x in enumerate((0, cells_x - 1)):
        copies.append(pltpu.make_async_copy(adjoint.at[:, x], ev.at[i], sems.at[i, 0]))
        copies.append(pltpu.make_async_copy(flags.at[x], gv.at[i], sems.at[i, 1]))
    for c in copies:
        c.start()
    pv[...] = pool_matrix(lanes)
    for f in range(fields):
        pp[f] = part[f]
    for c in copies:
        c.wait()
    for i, (face, at) in enumerate(((before, 0), (after, cells - rows))):
        for y in range(0, cells_y, 8):
            wgt = weight_of(gv[i, pl.ds(y, 8), :])
            for f in range(fields):
                wv[i, f, pl.ds(y, 8), :] = wgt * ev[i, f, pl.ds(y, 8), :] * face[f, pl.ds(y, 8), :]
        pooled = pooled_rows(wv.at[i], pv[...])
        for f in range(fields):
            pp[f, pl.ds(at + PAD, rows), :] = pp[f, pl.ds(at + PAD, rows), :] + pooled[f * rows : (f + 1) * rows]

    sub = lax.broadcasted_iota(jnp.int32, (8, lanes), 0)
    below = [None] + [sub < s for s in range(1, 8)]
    for t in range(per_dev):
        base = pl.multiple_of(slots[t] * tile_rows, 8)
        for v in range(tile_rows // 8):
            value = None
            for f in reversed(range(fields)):
                lo, hi = f * span - 8 * v, (f + 1) * span - 8 * v
                if hi <= 0 or lo >= 8:
                    continue
                piece = pp[f, pl.ds(PAD + span * t - lo, 8), :]
                value = piece if value is None else jnp.where(below[hi], piece, value)
            stage[pl.ds(t * tile_rows + 8 * v, 8), :] = value
        pltpu.make_async_copy(
            stage.at[pl.ds(t * tile_rows, tile_rows)], out.at[pl.ds(base, tile_rows)], tsem.at[0]
        ).start()
    pltpu.make_async_copy(stage, out.at[pl.ds(0, per_dev * tile_rows)], tsem.at[0]).wait()


def pack_part(part, slots, before, after, adjoint, flags, n_slots, tile_rows):
    fields, cells_x, cells_y, lanes = adjoint.shape
    f32 = jnp.float32
    vmem = pl.BlockSpec(memory_space=pltpu.VMEM)
    hbm = pl.BlockSpec(memory_space=pltpu.HBM)
    return pl.pallas_call(
        functools.partial(pack_kernel, tile_rows),
        out_shape=pltpu.HBM((n_slots * tile_rows, lanes), f32),
        in_specs=[pl.BlockSpec(memory_space=pltpu.SMEM), vmem, vmem, vmem, hbm, hbm],
        out_specs=hbm,
        scratch_shapes=[
            pltpu.VMEM((slots.shape[0] * tile_rows, lanes), f32),
            pltpu.VMEM(part.shape, f32),
            pltpu.VMEM((2, fields, cells_y, lanes), f32),
            pltpu.VMEM((2 * lanes, lanes), jnp.bfloat16),
            pltpu.VMEM((2, fields, cells_y, lanes), f32),
            pltpu.VMEM((2, cells_y, lanes), jnp.int32),
            pltpu.SemaphoreType.DMA((2, 2)),
            pltpu.SemaphoreType.DMA((1,)),
        ],
        compiler_params=pltpu.CompilerParams(vmem_limit_bytes=12 * MIB),
        cost_estimate=pl.CostEstimate(flops=1_000_000, bytes_accessed=3_500_000, transcendentals=0),
        name="edges_pack",
    )(slots, part, before, after, in_hbm(adjoint), in_hbm(flags))


def unpack_kernel(tile_rows, lookup, received, out, stage):
    fields, per_dev, width = out.shape
    lanes = received.shape[1]
    span = width // lanes

    for g in range(per_dev // 8):
        buf = stage.at[g % stage.shape[0]]
        for s in range(8):
            base = pl.multiple_of(lookup[g * 8 + s] * tile_rows, 8)
            buf[pl.ds(s * tile_rows, tile_rows), :] = received[pl.ds(base, tile_rows), :]
        for f in range(fields):
            for j in range(span):
                rows = buf[pl.ds(f * span + j, 8, stride=tile_rows), :]
                out[f, pl.ds(g * 8, 8), pl.ds(j * lanes, lanes)] = rows


def unpack_part(lookup, received, fields, per_dev, width, tile_rows):
    vmem = pl.BlockSpec(memory_space=pltpu.VMEM)
    lanes = received.shape[1]
    return pl.pallas_call(
        functools.partial(unpack_kernel, tile_rows),
        out_shape=jax.ShapeDtypeStruct((fields, per_dev, width), jnp.float32),
        in_specs=[pl.BlockSpec(memory_space=pltpu.SMEM), vmem],
        out_specs=vmem,
        scratch_shapes=[pltpu.VMEM((4, 8 * tile_rows, lanes), jnp.float32)],
        compiler_params=pltpu.CompilerParams(vmem_limit_bytes=8 * MIB),
        cost_estimate=pl.CostEstimate(flops=0, bytes_accessed=3_000_000, transcendentals=0),
        name="unpack",
    )(lookup, received)


def local(state, adjoint, source, kappa, cut_flags, coupling, target):
    state, adjoint, source, kappa, flags = (a[0] for a in (state, adjoint, source, kappa, cut_flags))
    fields, cells_x, cells_y, lanes = state.shape
    groups, bricks = lax.axis_size("grp"), lax.axis_size("brk")
    owners = groups * bricks
    per_dev = target.shape[1]
    capacity = per_dev // ((groups - 1) * bricks) + 1
    width = cells_x * cells_y * lanes // 8 // per_dev
    span = width // lanes
    tile_rows = -(-span * fields // 8) * 8
    myself = lax.axis_index(("grp", "brk"))

    up = [(i, i + 1) for i in range(bricks - 1)]
    down = [(j, i) for i, j in up]
    first, last = faces_of(state)
    before = lax.ppermute(last, "brk", up)
    after = lax.ppermute(first, "brk", down)

    part, slots = main_part(
        state, adjoint, source, kappa, flags, coupling, target, myself.reshape(1), capacity, span
    )
    outgoing = pack_part(part, slots, before, after, adjoint, flags, owners * capacity, tile_rows)
    outgoing = outgoing.reshape(owners, capacity * tile_rows, lanes)
    incoming = lax.all_to_all(outgoing, ("grp", "brk"), 0, 0, tiled=True)
    incoming = incoming.reshape(owners * capacity * tile_rows, lanes)

    slot_ids = myself * per_dev + jnp.arange(per_dev, dtype=jnp.int32)
    codes = jnp.arange(owners * per_dev, dtype=jnp.int32)
    hit = target.reshape(-1)[None, :] == slot_ids[:, None]
    origin = jnp.sum(jnp.where(hit, codes[None, :], 0), axis=1)
    sender = origin // per_dev
    before_it = jnp.logical_and(sender[:, None] == sender[None, :], origin[None, :] < origin[:, None])
    lookup = sender * capacity + jnp.sum(before_it.astype(jnp.int32), axis=1)
    out = unpack_part(lookup, incoming, fields, per_dev, width, tile_rows)
    return out.transpose(1, 0, 2)


def solution(mesh):
    placed = (
        P("grp", None, "brk", None, None),
        P("grp", None, "brk", None, None),
        P("grp", None, "brk", None, None),
        P("grp", "brk", None, None),
        P("grp", "brk", None, None),
        P(),
        P(),
    )
    return jax.shard_map(
        local, mesh=mesh, in_specs=placed, out_specs=P(("grp", "brk"), None, None), check_vma=False
    )
```

```python
import functools
import jax
import jax.numpy as jnp
from jax import lax
from jax.experimental import pallas as pl
from jax.experimental.pallas import tpu as pltpu
from jax.sharding import PartitionSpec as P

MIB = 1024 * 1024
PLANES = 4
AHEAD = 6
PAD = 8


def in_hbm(x):
    return pltpu.with_memory_space_constraint(x, pltpu.HBM)


def weight_of(flags):
    return 1.0 - 0.5 * flags.astype(jnp.float32)


def pool_matrix(lanes):
    row = lax.broadcasted_iota(jnp.int32, (2 * lanes, lanes), 0)
    col = lax.broadcasted_iota(jnp.int32, (2 * lanes, lanes), 1)
    return jnp.where(row // 2 == col, 1.0, 0.0).astype(jnp.bfloat16)


def pooled_rows(fine_ref, matrix):
    fields, cells_y, _ = fine_ref.shape
    rows = cells_y // 4
    parts = [[fine_ref[f, pl.ds(k, rows, stride=4), :] for k in range(4)] for f in range(fields)]
    low = jnp.concatenate([p[0] + p[1] for p in parts], axis=0)
    high = jnp.concatenate([p[2] + p[3] for p in parts], axis=0)
    both = jnp.concatenate([low, high], axis=1)
    first = both.astype(jnp.bfloat16)
    rest = both - first.astype(jnp.float32)
    second = rest.astype(jnp.bfloat16)
    dot = functools.partial(jnp.dot, preferred_element_type=jnp.float32)
    return dot(first, matrix) + dot(second, matrix)


def tile_values(load, fields, span, tile_rows, lanes):
    sub = lax.broadcasted_iota(jnp.int32, (8, lanes), 0)
    values = []
    for v in range(tile_rows // 8):
        value = None
        for f in reversed(range(fields)):
            lo, hi = f * span - 8 * v, (f + 1) * span - 8 * v
            if hi <= 0 or lo >= 8:
                continue
            piece = load(f, -lo)
            value = piece if value is None else jnp.where(sub < hi, piece, value)
        values.append(value)
    return values


def send_tile(slot, at, values, stage, out, tile_rows, sem):
    for v, value in enumerate(values):
        stage[pl.ds(pl.multiple_of(at * tile_rows + 8 * v, 8), 8), :] = value
    here = pl.ds(pl.multiple_of(at * tile_rows, 8), tile_rows)
    there = pl.ds(pl.multiple_of(slot * tile_rows, 8), tile_rows)
    pltpu.make_async_copy(stage.at[here], out.at[there], sem).start()


def await_tiles(first, count, stage, out, tile_rows, sem):
    rows = count * tile_rows
    pltpu.make_async_copy(stage.at[pl.ds(first * tile_rows, rows)], out.at[pl.ds(0, rows)], sem).wait()


def edge_tiles(rows, span):
    return -(-rows // span)


def face_kernel(state, first, last, sems):
    cells_x = state.shape[1]
    one = pltpu.make_async_copy(state.at[:, 0], first, sems.at[0])
    two = pltpu.make_async_copy(state.at[:, cells_x - 1], last, sems.at[1])
    one.start()
    two.start()
    one.wait()
    two.wait()


def faces_of(state):
    fields, _, cells_y, lanes = state.shape
    face = pltpu.HBM((fields, cells_y, lanes), jnp.float32)
    hbm = pl.BlockSpec(memory_space=pltpu.HBM)
    return pl.pallas_call(
        face_kernel,
        out_shape=(face, face),
        in_specs=[hbm],
        out_specs=(hbm, hbm),
        scratch_shapes=[pltpu.SemaphoreType.DMA((2,))],
        compiler_params=pltpu.CompilerParams(vmem_limit_bytes=2 * MIB),
        cost_estimate=pl.CostEstimate(flops=0, bytes_accessed=650_000, transcendentals=0),
        name="faces",
    )(in_hbm(state))


def main_kernel(
    capacity, span, tile_rows, myself, coupling, target, state, adjoint, source, kv, fv,
    sent, slots, ends, duals, out, stage, sv, av, bv, wv, pv, tv, seen, sems, tsem,
):
    fields, cells_x, cells_y, lanes = adjoint.shape
    steps = cells_x // PLANES
    rows = cells_y // 4
    owners, per_dev = target.shape

    def copy(step, i):
        at = pl.ds(PLANES * step, PLANES)
        if i == 0:
            landing = sv.at[:, pl.ds(PLANES * step + 1, PLANES), pl.ds(8, cells_y)]
            return pltpu.make_async_copy(state.at[:, at], landing, sems.at[step, 0])
        src, dst = ((adjoint, av), (source, bv))[i - 1]
        return pltpu.make_async_copy(src.at[:, at], dst.at[:, at], sems.at[step, i])

    def start(step):
        for i in range(3):
            copy(step, i).start()

    me = myself[0]
    row8 = pl.multiple_of(lax.shift_left(lax.shift_right_logical(me, 3), 3), 8)
    table = pltpu.make_async_copy(target.at[pl.ds(row8, 8)], tv, tsem.at[0])
    table.start()
    for step in range(AHEAD):
        start(step)
    zero = jnp.zeros((8, lanes), jnp.float32)
    pv[...] = pool_matrix(lanes)

    def clear(x, carry):
        for f in range(fields):
            sv[f, x, pl.ds(0, 8), :] = zero
            sv[f, x, pl.ds(cells_y + 8, 8), :] = zero
        return carry

    lax.fori_loop(0, cells_x + 2, clear, 0)
    for f in range(fields):
        for y in range(0, cells_y, 8):
            sv[f, 0, pl.ds(y + 8, 8), :] = zero
            sv[f, cells_x + 1, pl.ds(y + 8, 8), :] = zero

    for i in range(owners):
        seen[i] = 0
    table.wait()
    mine = lax.bitwise_and(me, 7)

    def rank(t, carry):
        owner = lax.shift_right_logical(tv[mine, t], per_dev.bit_length() - 1)
        count = seen[owner]
        slots[t] = owner * capacity + count
        seen[owner] = count + 1
        return carry

    lax.fori_loop(0, per_dev, rank, 0, unroll=8)

    coef = [[coupling[f, h] for h in range(fields)] for f in range(fields)]
    lane = lax.broadcasted_iota(jnp.int32, (8, lanes), 1)
    inner_lo = lane != 0
    inner_hi = lane != lanes - 1

    def pool(half, at):
        pooled = pooled_rows(wv.at[half], pv[...])
        for f in range(fields):
            out[f, pl.ds(pl.multiple_of(at + PAD, 8), rows), :] = pooled[f * rows : (f + 1) * rows]

    copy(0, 0).wait()
    edge = edge_tiles(rows, span)
    batch = PLANES // 2 * rows // span

    def place(first, count):
        for i in range(count):
            t = first + i
            values = tile_values(
                lambda f, d: out[f, pl.ds(PAD + span * t + d, 8), :], fields, span, tile_rows, lanes
            )
            send_tile(slots[t], t, values, stage, sent, tile_rows, tsem.at[1])

    def step_body(step, carry):
        @pl.when(step >= 2)
        def _():
            place(edge + batch * (step - 2), batch)

        @pl.when(step + AHEAD < steps)
        def _():
            start(step + AHEAD)

        @pl.when(step + 1 < steps)
        def _():
            copy(step + 1, 0).wait()

        copy(step, 1).wait()
        copy(step, 2).wait()

        for half in range(PLANES // 2):
            coarse = step * (PLANES // 2) + half
            pool(1 - half % 2, jnp.maximum(coarse - 1, 0) * rows)
            for y in range(0, cells_y, 8):
                total = [None] * fields
                for p in range(2):
                    x = 2 * coarse + p
                    kap = kv[x, pl.ds(y, 8), :]
                    wgt = weight_of(fv[x, pl.ds(y, 8), :])
                    mid = [sv[f, x + 1, pl.ds(y + 8, 8), :] for f in range(fields)]
                    for f in range(fields):
                        near = sv[f, x, pl.ds(y + 8, 8), :] + sv[f, x + 2, pl.ds(y + 8, 8), :]
                        near = near + sv[f, x + 1, pl.ds(y + 7, 8), :] + sv[f, x + 1, pl.ds(y + 9, 8), :]
                        near = near + jnp.where(inner_lo, pltpu.roll(mid[f], 1, 1), 0.0)
                        near = near + jnp.where(inner_hi, pltpu.roll(mid[f], lanes - 1, 1), 0.0)
                        applied = (kap + (coef[f][f] + 6.0)) * mid[f]
                        for h in range(fields):
                            if h != f:
                                applied = applied + coef[f][h] * mid[h]
                        residual = bv[f, x, pl.ds(y, 8), :] - applied + near
                        term = wgt * av[f, x, pl.ds(y, 8), :] * residual
                        total[f] = term if p == 0 else total[f] + term
                for f in range(fields):
                    wv[half % 2, f, pl.ds(y, 8), :] = total[f]
        return carry

    lax.fori_loop(0, steps, step_body, 0)
    pool(1, (cells_x // 2 - 1) * rows)
    done = edge + batch * (steps - 2)
    place(done, per_dev - edge - done)
    for i, x in enumerate((0, cells_x - 1)):
        for y in range(0, cells_y, 8):
            wgt = weight_of(fv[x, pl.ds(y, 8), :])
            for f in range(fields):
                duals[i, f, pl.ds(y, 8), :] = wgt * av[f, x, pl.ds(y, 8), :]
    kept = ends.shape[2]
    for f in range(fields):
        ends[0, f] = out[f, pl.ds(PAD, kept), :]
        ends[1, f] = out[f, pl.ds(PAD + per_dev * span - kept, kept), :]
    await_tiles(edge, per_dev - 2 * edge, stage, sent, tile_rows, tsem.at[1])


def main_part(state, adjoint, source, kappa, flags, coupling, target, myself, capacity, span, tile_rows):
    fields, cells_x, cells_y, lanes = state.shape
    owners, per_dev = target.shape
    kept = -(-edge_tiles(cells_y // 4, span) * span // 8) * 8
    f32 = jnp.float32
    hbm = pl.BlockSpec(memory_space=pltpu.HBM)
    vmem = pl.BlockSpec(memory_space=pltpu.VMEM)
    smem = pl.BlockSpec(memory_space=pltpu.SMEM)
    return pl.pallas_call(
        functools.partial(main_kernel, capacity, span, tile_rows),
        out_shape=(
            pltpu.HBM((owners * capacity * tile_rows, lanes), f32),
            jax.ShapeDtypeStruct((per_dev,), jnp.int32),
            pltpu.VMEM((2, fields, kept, lanes), f32),
            pltpu.VMEM((2, fields, cells_y, lanes), f32),
        ),
        in_specs=[smem, smem, hbm, hbm, hbm, hbm, vmem, vmem],
        out_specs=(hbm, smem, vmem, vmem),
        scratch_shapes=[
            pltpu.VMEM((fields, per_dev * span + 2 * PAD, lanes), f32),
            pltpu.VMEM((per_dev * tile_rows, lanes), f32),
            pltpu.VMEM((fields, cells_x + 2, cells_y + 16, lanes), f32),
            pltpu.VMEM((fields, cells_x, cells_y, lanes), f32),
            pltpu.VMEM((fields, cells_x, cells_y, lanes), f32),
            pltpu.VMEM((2, fields, cells_y, lanes), f32),
            pltpu.VMEM((2 * lanes, lanes), jnp.bfloat16),
            pltpu.SMEM((8, per_dev), jnp.int32),
            pltpu.SMEM((owners,), jnp.int32),
            pltpu.SemaphoreType.DMA((cells_x // PLANES, 3)),
            pltpu.SemaphoreType.DMA((2,)),
        ],
        compiler_params=pltpu.CompilerParams(vmem_limit_bytes=36 * MIB),
        cost_estimate=pl.CostEstimate(flops=100_000_000, bytes_accessed=27_700_000, transcendentals=0),
        name="residual_pool",
    )(myself, coupling, target, in_hbm(state), in_hbm(adjoint), in_hbm(source), kappa, flags)


def edge_kernel(span, tile_rows, slots, ends, duals, before, after, sent, out, stage, pe, wv, pv, sem):
    fields, cells_y, lanes = before.shape
    rows = cells_y // 4
    per_dev = slots.shape[0]
    kept = ends.shape[2]
    edge = edge_tiles(rows, span)
    pv[...] = pool_matrix(lanes)
    for i, (face, at) in enumerate(((before, 0), (after, kept - rows))):
        for y in range(0, cells_y, 8):
            for f in range(fields):
                wv[i, f, pl.ds(y, 8), :] = duals[i, f, pl.ds(y, 8), :] * face[f, pl.ds(y, 8), :]
        pooled = pooled_rows(wv.at[i], pv[...])
        for f in range(fields):
            pe[i, f, pl.ds(PAD, kept), :] = ends[i, f]
            here = pl.ds(at + PAD, rows)
            pe[i, f, here, :] = pe[i, f, here, :] + pooled[f * rows : (f + 1) * rows]
    for i, (tile, start) in enumerate(((0, 0), (per_dev - edge, kept - edge * span))):
        for k in range(edge):
            values = tile_values(
                lambda f, d: pe[i, f, pl.ds(PAD + start + span * k + d, 8), :], fields, span, tile_rows, lanes
            )
            send_tile(slots[tile + k], i * edge + k, values, stage, out, tile_rows, sem.at[0])
    await_tiles(0, 2 * edge, stage, out, tile_rows, sem.at[0])


def edge_part(sent, slots, ends, duals, before, after, span, tile_rows):
    fields, cells_y, lanes = before.shape
    f32 = jnp.float32
    vmem = pl.BlockSpec(memory_space=pltpu.VMEM)
    hbm = pl.BlockSpec(memory_space=pltpu.HBM)
    edge = edge_tiles(cells_y // 4, span)
    return pl.pallas_call(
        functools.partial(edge_kernel, span, tile_rows),
        out_shape=pltpu.HBM(sent.shape, f32),
        in_specs=[pl.BlockSpec(memory_space=pltpu.SMEM), vmem, vmem, vmem, vmem, hbm],
        out_specs=hbm,
        scratch_shapes=[
            pltpu.VMEM((2 * edge * tile_rows, lanes), f32),
            pltpu.VMEM((2, fields, ends.shape[2] + 2 * PAD, lanes), f32),
            pltpu.VMEM((2, fields, cells_y, lanes), f32),
            pltpu.VMEM((2 * lanes, lanes), jnp.bfloat16),
            pltpu.SemaphoreType.DMA((1,)),
        ],
        input_output_aliases={5: 0},
        compiler_params=pltpu.CompilerParams(vmem_limit_bytes=12 * MIB),
        cost_estimate=pl.CostEstimate(flops=1_000_000, bytes_accessed=100_000, transcendentals=0),
        name="edges",
    )(slots, ends, duals, before, after, in_hbm(sent))


def unpack_kernel(tile_rows, lookup, received, out, stage, built, sems):
    fields, per_dev, width = built.shape
    lanes = received.shape[1]
    span = width // lanes
    piece = per_dev // sems.shape[0]

    def leave(k):
        here = pl.ds(k * piece, piece)
        return pltpu.make_async_copy(built.at[:, here], out.at[:, here], sems.at[k])

    for g in range(per_dev // 8):
        buf = stage.at[g % stage.shape[0]]
        for s in range(8):
            base = pl.multiple_of(lookup[g * 8 + s] * tile_rows, 8)
            buf[pl.ds(s * tile_rows, tile_rows), :] = received[pl.ds(base, tile_rows), :]
        for f in range(fields):
            for j in range(span):
                rows = buf[pl.ds(f * span + j, 8, stride=tile_rows), :]
                built[f, pl.ds(g * 8, 8), pl.ds(j * lanes, lanes)] = rows
        if (g + 1) * 8 % piece == 0:
            leave(g * 8 // piece).start()
    for k in range(sems.shape[0]):
        leave(k).wait()


def unpack_part(lookup, received, fields, per_dev, width, tile_rows):
    lanes = received.shape[1]
    return pl.pallas_call(
        functools.partial(unpack_kernel, tile_rows),
        out_shape=jax.ShapeDtypeStruct((fields, per_dev, width), jnp.float32),
        in_specs=[pl.BlockSpec(memory_space=pltpu.SMEM), pl.BlockSpec(memory_space=pltpu.VMEM)],
        out_specs=pl.BlockSpec(memory_space=pltpu.HBM),
        scratch_shapes=[
            pltpu.VMEM((4, 8 * tile_rows, lanes), jnp.float32),
            pltpu.VMEM((fields, per_dev, width), jnp.float32),
            pltpu.SemaphoreType.DMA((4,)),
        ],
        compiler_params=pltpu.CompilerParams(vmem_limit_bytes=8 * MIB),
        cost_estimate=pl.CostEstimate(flops=0, bytes_accessed=3_000_000, transcendentals=0),
        name="unpack",
    )(lookup, received)


def local(state, adjoint, source, kappa, cut_flags, coupling, target):
    state, adjoint, source, kappa, flags = (a[0] for a in (state, adjoint, source, kappa, cut_flags))
    fields, cells_x, cells_y, lanes = state.shape
    groups, bricks = lax.axis_size("grp"), lax.axis_size("brk")
    owners = groups * bricks
    per_dev = target.shape[1]
    capacity = per_dev // ((groups - 1) * bricks) + 1
    width = cells_x * cells_y * lanes // 8 // per_dev
    span = width // lanes
    tile_rows = -(-span * fields // 8) * 8
    myself = lax.axis_index(("grp", "brk"))

    up = [(i, i + 1) for i in range(bricks - 1)]
    down = [(j, i) for i, j in up]
    first, last = faces_of(state)
    before = lax.ppermute(last, "brk", up)
    after = lax.ppermute(first, "brk", down)

    sent, slots, ends, duals = main_part(
        state, adjoint, source, kappa, flags, coupling, target, myself.reshape(1), capacity, span, tile_rows
    )
    outgoing = edge_part(sent, slots, ends, duals, before, after, span, tile_rows)
    outgoing = outgoing.reshape(owners, capacity * tile_rows, lanes)
    incoming = lax.all_to_all(outgoing, ("grp", "brk"), 0, 0, tiled=True)
    incoming = incoming.reshape(owners * capacity * tile_rows, lanes)

    slot_ids = myself * per_dev + jnp.arange(per_dev, dtype=jnp.int32)
    codes = jnp.arange(owners * per_dev, dtype=jnp.int32)
    hit = target.reshape(-1)[None, :] == slot_ids[:, None]
    origin = jnp.sum(jnp.where(hit, codes[None, :], 0), axis=1)
    sender = origin // per_dev
    before_it = jnp.logical_and(sender[:, None] == sender[None, :], origin[None, :] < origin[:, None])
    lookup = sender * capacity + jnp.sum(before_it.astype(jnp.int32), axis=1)
    out = unpack_part(lookup, incoming, fields, per_dev, width, tile_rows)
    return out.transpose(1, 0, 2)


def solution(mesh):
    placed = (
        P("grp", None, "brk", None, None),
        P("grp", None, "brk", None, None),
        P("grp", None, "brk", None, None),
        P("grp", "brk", None, None),
        P("grp", "brk", None, None),
        P(),
        P(),
    )
    return jax.shard_map(
        local, mesh=mesh, in_specs=placed, out_specs=P(("grp", "brk"), None, None), check_vma=False
    )
```

```python
import functools
import jax
import jax.numpy as jnp
from jax import lax
from jax.experimental import pallas as pl
from jax.experimental.pallas import tpu as pltpu
from jax.sharding import PartitionSpec as P

MIB = 1024 * 1024
PLANES = 4
AHEAD = 12
PAD = 8


def in_hbm(x):
    return pltpu.with_memory_space_constraint(x, pltpu.HBM)


def weight_of(flags):
    return 1.0 - 0.5 * flags.astype(jnp.float32)


def pool_matrix(lanes):
    row = lax.broadcasted_iota(jnp.int32, (2 * lanes, lanes), 0)
    col = lax.broadcasted_iota(jnp.int32, (2 * lanes, lanes), 1)
    return jnp.where(row // 2 == col, 1.0, 0.0).astype(jnp.bfloat16)


def pooled_rows(fine_ref, matrix):
    fields, cells_y, _ = fine_ref.shape
    rows = cells_y // 4
    parts = [[fine_ref[f, pl.ds(k, rows, stride=4), :] for k in range(4)] for f in range(fields)]
    low = jnp.concatenate([p[0] + p[1] for p in parts], axis=0)
    high = jnp.concatenate([p[2] + p[3] for p in parts], axis=0)
    both = jnp.concatenate([low, high], axis=1)
    first = both.astype(jnp.bfloat16)
    rest = both - first.astype(jnp.float32)
    second = rest.astype(jnp.bfloat16)
    dot = functools.partial(jnp.dot, preferred_element_type=jnp.float32)
    return dot(first, matrix) + dot(second, matrix)


def tile_values(load, fields, span, tile_rows, lanes):
    sub = lax.broadcasted_iota(jnp.int32, (8, lanes), 0)
    values = []
    for v in range(tile_rows // 8):
        value = None
        for f in reversed(range(fields)):
            lo, hi = f * span - 8 * v, (f + 1) * span - 8 * v
            if hi <= 0 or lo >= 8:
                continue
            piece = load(f, -lo)
            value = piece if value is None else jnp.where(sub < hi, piece, value)
        values.append(value)
    return values


def send_tile(slot, at, values, stage, out, tile_rows, sem):
    for v, value in enumerate(values):
        stage[pl.ds(pl.multiple_of(at * tile_rows + 8 * v, 8), 8), :] = value
    here = pl.ds(pl.multiple_of(at * tile_rows, 8), tile_rows)
    there = pl.ds(pl.multiple_of(slot * tile_rows, 8), tile_rows)
    pltpu.make_async_copy(stage.at[here], out.at[there], sem).start()


def await_tiles(first, count, stage, out, tile_rows, sem):
    rows = count * tile_rows
    pltpu.make_async_copy(stage.at[pl.ds(first * tile_rows, rows)], out.at[pl.ds(0, rows)], sem).wait()


def edge_tiles(rows, span):
    return -(-rows // span)


def face_kernel(odd, state, inner, outer, sems):
    end = state.shape[1] - 1
    one = pltpu.make_async_copy(state.at[:, end - end * odd[0]], inner, sems.at[0])
    two = pltpu.make_async_copy(state.at[:, end * odd[0]], outer, sems.at[1])
    one.start()
    two.start()
    one.wait()
    two.wait()


def faces_of(state, odd):
    fields, _, cells_y, lanes = state.shape
    face = jax.ShapeDtypeStruct((fields, cells_y, lanes), jnp.float32)
    vmem = pl.BlockSpec(memory_space=pltpu.VMEM)
    return pl.pallas_call(
        face_kernel,
        out_shape=(face, face),
        in_specs=[pl.BlockSpec(memory_space=pltpu.SMEM), pl.BlockSpec(memory_space=pltpu.HBM)],
        out_specs=(vmem, vmem),
        scratch_shapes=[pltpu.SemaphoreType.DMA((2,))],
        compiler_params=pltpu.CompilerParams(vmem_limit_bytes=2 * MIB),
        cost_estimate=pl.CostEstimate(flops=0, bytes_accessed=650_000, transcendentals=0),
        name="faces",
    )(odd.reshape(1), in_hbm(state))


def main_kernel(
    capacity, myself, coupling, target, state, adjoint, source, kv, fv,
    out, slots, duals, sv, av, bv, wv, pv, tv, seen, sems, tsem,
):
    fields, cells_x, cells_y, lanes = adjoint.shape
    steps = cells_x // PLANES
    rows = cells_y // 4
    owners, per_dev = target.shape

    def copy(step, i):
        at = pl.ds(PLANES * step, PLANES)
        if i == 0:
            landing = sv.at[:, pl.ds(PLANES * step + 1, PLANES), pl.ds(8, cells_y)]
            return pltpu.make_async_copy(state.at[:, at], landing, sems.at[step, 0])
        src, dst = ((adjoint, av), (source, bv))[i - 1]
        return pltpu.make_async_copy(src.at[:, at], dst.at[:, at], sems.at[step, i])

    def start(step):
        for i in range(3):
            copy(step, i).start()

    me = myself[0]
    row8 = pl.multiple_of(lax.shift_left(lax.shift_right_logical(me, 3), 3), 8)
    table = pltpu.make_async_copy(target.at[pl.ds(row8, 8)], tv, tsem.at[0])
    table.start()
    for step in range(AHEAD):
        start(step)
    zero = jnp.zeros((8, lanes), jnp.float32)
    pv[...] = pool_matrix(lanes)

    def clear(x, carry):
        for f in range(fields):
            sv[f, x, pl.ds(0, 8), :] = zero
            sv[f, x, pl.ds(cells_y + 8, 8), :] = zero
        return carry

    lax.fori_loop(0, cells_x + 2, clear, 0)
    for f in range(fields):
        for y in range(0, cells_y, 8):
            sv[f, 0, pl.ds(y + 8, 8), :] = zero
            sv[f, cells_x + 1, pl.ds(y + 8, 8), :] = zero

    for i in range(owners):
        seen[i] = 0
    table.wait()
    mine = lax.bitwise_and(me, 7)

    def rank(t, carry):
        owner = lax.shift_right_logical(tv[mine, t], per_dev.bit_length() - 1)
        count = seen[owner]
        slots[t] = owner * capacity + count
        seen[owner] = count + 1
        return carry

    lax.fori_loop(0, per_dev, rank, 0, unroll=8)

    coef = [[coupling[f, h] for h in range(fields)] for f in range(fields)]
    lane = lax.broadcasted_iota(jnp.int32, (8, lanes), 1)
    inner_lo = lane != 0
    inner_hi = lane != lanes - 1

    def pool(half, at):
        pooled = pooled_rows(wv.at[half], pv[...])
        for f in range(fields):
            out[f, pl.ds(pl.multiple_of(at + PAD, 8), rows), :] = pooled[f * rows : (f + 1) * rows]

    copy(0, 0).wait()
    def step_body(step, carry):
        @pl.when(step + AHEAD < steps)
        def _():
            start(step + AHEAD)

        @pl.when(step + 1 < steps)
        def _():
            copy(step + 1, 0).wait()

        copy(step, 1).wait()
        copy(step, 2).wait()

        for half in range(PLANES // 2):
            coarse = step * (PLANES // 2) + half
            pool(1 - half % 2, jnp.maximum(coarse - 1, 0) * rows)
            for y in range(0, cells_y, 8):
                total = [None] * fields
                for p in range(2):
                    x = 2 * coarse + p
                    kap = kv[x, pl.ds(y, 8), :]
                    wgt = weight_of(fv[x, pl.ds(y, 8), :])
                    mid = [sv[f, x + 1, pl.ds(y + 8, 8), :] for f in range(fields)]
                    for f in range(fields):
                        near = sv[f, x, pl.ds(y + 8, 8), :] + sv[f, x + 2, pl.ds(y + 8, 8), :]
                        near = near + sv[f, x + 1, pl.ds(y + 7, 8), :] + sv[f, x + 1, pl.ds(y + 9, 8), :]
                        near = near + jnp.where(inner_lo, pltpu.roll(mid[f], 1, 1), 0.0)
                        near = near + jnp.where(inner_hi, pltpu.roll(mid[f], lanes - 1, 1), 0.0)
                        applied = (kap + (coef[f][f] + 6.0)) * mid[f]
                        for h in range(fields):
                            if h != f:
                                applied = applied + coef[f][h] * mid[h]
                        residual = bv[f, x, pl.ds(y, 8), :] - applied + near
                        term = wgt * av[f, x, pl.ds(y, 8), :] * residual
                        total[f] = term if p == 0 else total[f] + term
                for f in range(fields):
                    wv[half % 2, f, pl.ds(y, 8), :] = total[f]
        return carry

    lax.fori_loop(0, steps, step_body, 0)
    pool(1, (cells_x // 2 - 1) * rows)
    for i, x in enumerate((0, cells_x - 1)):
        for y in range(0, cells_y, 8):
            wgt = weight_of(fv[x, pl.ds(y, 8), :])
            for f in range(fields):
                duals[i, f, pl.ds(y, 8), :] = wgt * av[f, x, pl.ds(y, 8), :]

def main_part(state, adjoint, source, kappa, flags, coupling, target, myself, capacity):
    fields, cells_x, cells_y, lanes = state.shape
    owners, per_dev = target.shape
    f32 = jnp.float32
    hbm = pl.BlockSpec(memory_space=pltpu.HBM)
    vmem = pl.BlockSpec(memory_space=pltpu.VMEM)
    smem = pl.BlockSpec(memory_space=pltpu.SMEM)
    return pl.pallas_call(
        functools.partial(main_kernel, capacity),
        out_shape=(
            jax.ShapeDtypeStruct((fields, cells_x * cells_y // 8 + 2 * PAD, lanes), f32),
            jax.ShapeDtypeStruct((per_dev,), jnp.int32),
            jax.ShapeDtypeStruct((2, fields, cells_y, lanes), f32),
        ),
        in_specs=[smem, smem, hbm, hbm, hbm, hbm, vmem, vmem],
        out_specs=(vmem, smem, vmem),
        scratch_shapes=[
            pltpu.VMEM((fields, cells_x + 2, cells_y + 16, lanes), f32),
            pltpu.VMEM((fields, cells_x, cells_y, lanes), f32),
            pltpu.VMEM((fields, cells_x, cells_y, lanes), f32),
            pltpu.VMEM((2, fields, cells_y, lanes), f32),
            pltpu.VMEM((2 * lanes, lanes), jnp.bfloat16),
            pltpu.SMEM((8, per_dev), jnp.int32),
            pltpu.SMEM((owners,), jnp.int32),
            pltpu.SemaphoreType.DMA((cells_x // PLANES, 3)),
            pltpu.SemaphoreType.DMA((1,)),
        ],
        compiler_params=pltpu.CompilerParams(vmem_limit_bytes=36 * MIB),
        cost_estimate=pl.CostEstimate(flops=100_000_000, bytes_accessed=27_700_000, transcendentals=0),
        name="residual_pool",
    )(myself, coupling, target, in_hbm(state), in_hbm(adjoint), in_hbm(source), kappa, flags)


def pack_kernel(tile_rows, odd, slots, part, duals, inner, outer, out, stage, pe, wv, pv, sem):
    fields, cells_y, lanes = inner.shape
    rows = cells_y // 4
    per_dev = slots.shape[0]
    cells = part.shape[1] - 2 * PAD
    span = cells // per_dev
    kept = pe.shape[2] - 2 * PAD
    edge = edge_tiles(rows, span)
    pv[...] = pool_matrix(lanes)
    swapped = odd[0] != 0
    for f in range(fields):
        for y in range(0, cells_y, 8):
            here = pl.ds(y, 8)
            near, far = inner[f, here, :], outer[f, here, :]
            wv[0, f, here, :] = duals[0, f, here, :] * jnp.where(swapped, near, far)
            wv[1, f, here, :] = duals[1, f, here, :] * jnp.where(swapped, far, near)
    pooled = [pooled_rows(wv.at[i], pv[...]) for i in range(2)]
    for t in range(edge, per_dev - edge):
        values = tile_values(
            lambda f, d: part[f, pl.ds(PAD + span * t + d, 8), :], fields, span, tile_rows, lanes
        )
        send_tile(slots[t], t, values, stage, out, tile_rows, sem.at[0])
    for i, (at, start) in enumerate(((0, 0), (kept - rows, cells - kept))):
        for f in range(fields):
            pe[i, f, pl.ds(PAD, kept), :] = part[f, pl.ds(PAD + start, kept), :]
            here = pl.ds(at + PAD, rows)
            pe[i, f, here, :] = pe[i, f, here, :] + pooled[i][f * rows : (f + 1) * rows]
    for i, (tile, start) in enumerate(((0, 0), (per_dev - edge, kept - edge * span))):
        for k in range(edge):
            values = tile_values(
                lambda f, d: pe[i, f, pl.ds(PAD + start + span * k + d, 8), :], fields, span, tile_rows, lanes
            )
            send_tile(slots[tile + k], tile + k, values, stage, out, tile_rows, sem.at[0])
    await_tiles(0, per_dev, stage, out, tile_rows, sem.at[0])


def pack_part(odd, part, slots, duals, inner, outer, n_slots, tile_rows):
    fields, cells_y, lanes = inner.shape
    per_dev = slots.shape[0]
    span = (part.shape[1] - 2 * PAD) // per_dev
    kept = -(-edge_tiles(cells_y // 4, span) * span // 8) * 8
    f32 = jnp.float32
    vmem = pl.BlockSpec(memory_space=pltpu.VMEM)
    return pl.pallas_call(
        functools.partial(pack_kernel, tile_rows),
        out_shape=pltpu.HBM((n_slots * tile_rows, lanes), f32),
        in_specs=[pl.BlockSpec(memory_space=pltpu.SMEM)] * 2 + [vmem] * 4,
        out_specs=pl.BlockSpec(memory_space=pltpu.HBM),
        scratch_shapes=[
            pltpu.VMEM((per_dev * tile_rows, lanes), f32),
            pltpu.VMEM((2, fields, kept + 2 * PAD, lanes), f32),
            pltpu.VMEM((2, fields, cells_y, lanes), f32),
            pltpu.VMEM((2 * lanes, lanes), jnp.bfloat16),
            pltpu.SemaphoreType.DMA((1,)),
        ],
        compiler_params=pltpu.CompilerParams(vmem_limit_bytes=12 * MIB),
        cost_estimate=pl.CostEstimate(flops=1_000_000, bytes_accessed=3_500_000, transcendentals=0),
        name="edges_pack",
    )(odd, slots, part, duals, inner, outer)


def unpack_kernel(tile_rows, lookup, received, out, stage, built, sems):
    fields, per_dev, width = built.shape
    lanes = received.shape[1]
    span = width // lanes
    piece = per_dev // sems.shape[0]

    def leave(k):
        here = pl.ds(k * piece, piece)
        return pltpu.make_async_copy(built.at[:, here], out.at[:, here], sems.at[k])

    for g in range(per_dev // 8):
        buf = stage.at[g % stage.shape[0]]
        for s in range(8):
            base = pl.multiple_of(lookup[g * 8 + s] * tile_rows, 8)
            buf[pl.ds(s * tile_rows, tile_rows), :] = received[pl.ds(base, tile_rows), :]
        for f in range(fields):
            for j in range(span):
                rows = buf[pl.ds(f * span + j, 8, stride=tile_rows), :]
                built[f, pl.ds(g * 8, 8), pl.ds(j * lanes, lanes)] = rows
        if (g + 1) * 8 % piece == 0:
            leave(g * 8 // piece).start()
    for k in range(sems.shape[0]):
        leave(k).wait()


def unpack_part(lookup, received, fields, per_dev, width, tile_rows):
    lanes = received.shape[1]
    return pl.pallas_call(
        functools.partial(unpack_kernel, tile_rows),
        out_shape=jax.ShapeDtypeStruct((fields, per_dev, width), jnp.float32),
        in_specs=[pl.BlockSpec(memory_space=pltpu.SMEM), pl.BlockSpec(memory_space=pltpu.VMEM)],
        out_specs=pl.BlockSpec(memory_space=pltpu.HBM),
        scratch_shapes=[
            pltpu.VMEM((4, 8 * tile_rows, lanes), jnp.float32),
            pltpu.VMEM((fields, per_dev, width), jnp.float32),
            pltpu.SemaphoreType.DMA((4,)),
        ],
        compiler_params=pltpu.CompilerParams(vmem_limit_bytes=8 * MIB),
        cost_estimate=pl.CostEstimate(flops=0, bytes_accessed=3_000_000, transcendentals=0),
        name="unpack",
    )(lookup, received)


def local(state, adjoint, source, kappa, cut_flags, coupling, target):
    state, adjoint, source, kappa, flags = (a[0] for a in (state, adjoint, source, kappa, cut_flags))
    fields, cells_x, cells_y, lanes = state.shape
    groups, bricks = lax.axis_size("grp"), lax.axis_size("brk")
    owners = groups * bricks
    per_dev = target.shape[1]
    capacity = per_dev // ((groups - 1) * bricks) + 1
    width = cells_x * cells_y * lanes // 8 // per_dev
    span = width // lanes
    tile_rows = -(-span * fields // 8) * 8
    myself = lax.axis_index(("grp", "brk"))

    odd = lax.rem(lax.axis_index("brk"), 2)
    one = [(i, i ^ 1) for i in range(bricks)]
    two = [(i, j) for i in range(1, bricks - 1) for j in (((i - 1) ^ 1) + 1,)]
    faces = faces_of(state, odd)
    inner = lax.ppermute(faces[0], "brk", one)
    outer = lax.ppermute(faces[1], "brk", two)

    part, slots, duals = main_part(
        state, adjoint, source, kappa, flags, coupling, target, myself.reshape(1), capacity
    )
    outgoing = pack_part(odd.reshape(1), part, slots, duals, inner, outer, owners * capacity, tile_rows)
    outgoing = outgoing.reshape(owners, capacity * tile_rows, lanes)
    incoming = lax.all_to_all(outgoing, ("grp", "brk"), 0, 0, tiled=True)
    incoming = incoming.reshape(owners * capacity * tile_rows, lanes)

    slot_ids = myself * per_dev + jnp.arange(per_dev, dtype=jnp.int32)
    codes = jnp.arange(owners * per_dev, dtype=jnp.int32)
    hit = target.reshape(-1)[None, :] == slot_ids[:, None]
    origin = jnp.sum(jnp.where(hit, codes[None, :], 0), axis=1)
    sender = origin // per_dev
    before_it = jnp.logical_and(sender[:, None] == sender[None, :], origin[None, :] < origin[:, None])
    lookup = sender * capacity + jnp.sum(before_it.astype(jnp.int32), axis=1)
    out = unpack_part(lookup, incoming, fields, per_dev, width, tile_rows)
    return out.transpose(1, 0, 2)


def solution(mesh):
    placed = (
        P("grp", None, "brk", None, None),
        P("grp", None, "brk", None, None),
        P("grp", None, "brk", None, None),
        P("grp", "brk", None, None),
        P("grp", "brk", None, None),
        P(),
        P(),
    )
    return jax.shard_map(
        local, mesh=mesh, in_specs=placed, out_specs=P(("grp", "brk"), None, None), check_vma=False
    )
```

```python
import functools
import jax
import jax.numpy as jnp
from jax import lax
from jax.experimental import pallas as pl
from jax.experimental.pallas import tpu as pltpu
from jax.sharding import PartitionSpec as P

MIB = 1024 * 1024
PLANES = 4
AHEAD = 12
PAD = 8


def in_hbm(x):
    return pltpu.with_memory_space_constraint(x, pltpu.HBM)


def weight_of(flags):
    return 1.0 - 0.5 * flags.astype(jnp.float32)


def pool_matrix(lanes):
    row = lax.broadcasted_iota(jnp.int32, (2 * lanes, lanes), 0)
    col = lax.broadcasted_iota(jnp.int32, (2 * lanes, lanes), 1)
    return jnp.where(row // 2 == col, 1.0, 0.0).astype(jnp.bfloat16)


def pooled_rows(fine_ref, matrix):
    fields, cells_y, _ = fine_ref.shape
    rows = cells_y // 4
    parts = [[fine_ref[f, pl.ds(k, rows, stride=4), :] for k in range(4)] for f in range(fields)]
    low = jnp.concatenate([p[0] + p[1] for p in parts], axis=0)
    high = jnp.concatenate([p[2] + p[3] for p in parts], axis=0)
    both = jnp.concatenate([low, high], axis=1)
    first = both.astype(jnp.bfloat16)
    rest = both - first.astype(jnp.float32)
    second = rest.astype(jnp.bfloat16)
    dot = functools.partial(jnp.dot, preferred_element_type=jnp.float32)
    return dot(first, matrix) + dot(second, matrix)


def tile_values(load, fields, span, tile_rows, lanes):
    sub = lax.broadcasted_iota(jnp.int32, (8, lanes), 0)
    values = []
    for v in range(tile_rows // 8):
        value = None
        for f in reversed(range(fields)):
            lo, hi = f * span - 8 * v, (f + 1) * span - 8 * v
            if hi <= 0 or lo >= 8:
                continue
            piece = load(f, -lo)
            value = piece if value is None else jnp.where(sub < hi, piece, value)
        values.append(value)
    return values


def send_tile(slot, at, values, stage, out, tile_rows, sem):
    for v, value in enumerate(values):
        stage[pl.ds(pl.multiple_of(at * tile_rows + 8 * v, 8), 8), :] = value
    here = pl.ds(pl.multiple_of(at * tile_rows, 8), tile_rows)
    there = pl.ds(pl.multiple_of(slot * tile_rows, 8), tile_rows)
    pltpu.make_async_copy(stage.at[here], out.at[there], sem).start()


def await_tiles(first, count, stage, out, tile_rows, sem):
    rows = count * tile_rows
    pltpu.make_async_copy(stage.at[pl.ds(first * tile_rows, rows)], out.at[pl.ds(0, rows)], sem).wait()


def edge_tiles(rows, span):
    return -(-rows // span)


def face_kernel(state, first, last, sems):
    cells_x = state.shape[1]
    one = pltpu.make_async_copy(state.at[:, 0], first, sems.at[0])
    two = pltpu.make_async_copy(state.at[:, cells_x - 1], last, sems.at[1])
    one.start()
    two.start()
    one.wait()
    two.wait()


def faces_of(state):
    fields, _, cells_y, lanes = state.shape
    face = jax.ShapeDtypeStruct((fields, cells_y, lanes), jnp.float32)
    vmem = pl.BlockSpec(memory_space=pltpu.VMEM)
    return pl.pallas_call(
        face_kernel,
        out_shape=(face, face),
        in_specs=[pl.BlockSpec(memory_space=pltpu.HBM)],
        out_specs=(vmem, vmem),
        scratch_shapes=[pltpu.SemaphoreType.DMA((2,))],
        compiler_params=pltpu.CompilerParams(vmem_limit_bytes=2 * MIB),
        cost_estimate=pl.CostEstimate(flops=0, bytes_accessed=650_000, transcendentals=0),
        name="faces",
    )(in_hbm(state))


def main_kernel(
    capacity, myself, coupling, target, state, adjoint, source, kappa, flags,
    out, slots, duals, sv, av, bv, kv, fv, wv, pv, tv, seen, sems, tsem,
):
    fields, cells_x, cells_y, lanes = adjoint.shape
    steps = cells_x // PLANES
    rows = cells_y // 4
    owners, per_dev = target.shape

    def copy(step, i):
        at = pl.ds(PLANES * step, PLANES)
        if i == 0:
            landing = sv.at[:, pl.ds(PLANES * step + 1, PLANES), pl.ds(8, cells_y)]
            return pltpu.make_async_copy(state.at[:, at], landing, sems.at[step, 0])
        if i > 2:
            src, dst = ((kappa, kv), (flags, fv))[i - 3]
            return pltpu.make_async_copy(src.at[at], dst.at[at], sems.at[step, i])
        src, dst = ((adjoint, av), (source, bv))[i - 1]
        return pltpu.make_async_copy(src.at[:, at], dst.at[:, at], sems.at[step, i])

    def start(step):
        for i in range(5):
            copy(step, i).start()

    me = myself[0]
    row8 = pl.multiple_of(lax.shift_left(lax.shift_right_logical(me, 3), 3), 8)
    table = pltpu.make_async_copy(target.at[pl.ds(row8, 8)], tv, tsem.at[0])
    table.start()
    for step in range(AHEAD):
        start(step)
    zero = jnp.zeros((8, lanes), jnp.float32)
    pv[...] = pool_matrix(lanes)

    def clear(x, carry):
        for f in range(fields):
            sv[f, x, pl.ds(0, 8), :] = zero
            sv[f, x, pl.ds(cells_y + 8, 8), :] = zero
        return carry

    lax.fori_loop(0, cells_x + 2, clear, 0)
    for f in range(fields):
        for y in range(0, cells_y, 8):
            sv[f, 0, pl.ds(y + 8, 8), :] = zero
            sv[f, cells_x + 1, pl.ds(y + 8, 8), :] = zero

    for i in range(owners):
        seen[i] = 0
    table.wait()
    mine = lax.bitwise_and(me, 7)

    def rank(t, carry):
        owner = lax.shift_right_logical(tv[mine, t], per_dev.bit_length() - 1)
        count = seen[owner]
        slots[t] = owner * capacity + count
        seen[owner] = count + 1
        return carry

    lax.fori_loop(0, per_dev, rank, 0, unroll=8)

    coef = [[coupling[f, h] for h in range(fields)] for f in range(fields)]
    lane = lax.broadcasted_iota(jnp.int32, (8, lanes), 1)
    inner_lo = lane != 0
    inner_hi = lane != lanes - 1

    def pool(half, at):
        pooled = pooled_rows(wv.at[half], pv[...])
        for f in range(fields):
            out[f, pl.ds(pl.multiple_of(at + PAD, 8), rows), :] = pooled[f * rows : (f + 1) * rows]

    copy(0, 0).wait()
    def step_body(step, carry):
        @pl.when(step + AHEAD < steps)
        def _():
            start(step + AHEAD)

        @pl.when(step + 1 < steps)
        def _():
            copy(step + 1, 0).wait()

        for i in range(1, 5):
            copy(step, i).wait()

        for half in range(PLANES // 2):
            coarse = step * (PLANES // 2) + half
            pool(1 - half % 2, jnp.maximum(coarse - 1, 0) * rows)
            for y in range(0, cells_y, 8):
                total = [None] * fields
                for p in range(2):
                    x = 2 * coarse + p
                    kap = kv[x, pl.ds(y, 8), :]
                    wgt = weight_of(fv[x, pl.ds(y, 8), :])
                    mid = [sv[f, x + 1, pl.ds(y + 8, 8), :] for f in range(fields)]
                    for f in range(fields):
                        near = sv[f, x, pl.ds(y + 8, 8), :] + sv[f, x + 2, pl.ds(y + 8, 8), :]
                        near = near + sv[f, x + 1, pl.ds(y + 7, 8), :] + sv[f, x + 1, pl.ds(y + 9, 8), :]
                        near = near + jnp.where(inner_lo, pltpu.roll(mid[f], 1, 1), 0.0)
                        near = near + jnp.where(inner_hi, pltpu.roll(mid[f], lanes - 1, 1), 0.0)
                        applied = (kap + (coef[f][f] + 6.0)) * mid[f]
                        for h in range(fields):
                            if h != f:
                                applied = applied + coef[f][h] * mid[h]
                        residual = bv[f, x, pl.ds(y, 8), :] - applied + near
                        term = wgt * av[f, x, pl.ds(y, 8), :] * residual
                        total[f] = term if p == 0 else total[f] + term
                for f in range(fields):
                    wv[half % 2, f, pl.ds(y, 8), :] = total[f]
        return carry

    lax.fori_loop(0, steps, step_body, 0)
    pool(1, (cells_x // 2 - 1) * rows)
    for i, x in enumerate((0, cells_x - 1)):
        for y in range(0, cells_y, 8):
            wgt = weight_of(fv[x, pl.ds(y, 8), :])
            for f in range(fields):
                duals[i, f, pl.ds(y, 8), :] = wgt * av[f, x, pl.ds(y, 8), :]

def main_part(state, adjoint, source, kappa, flags, coupling, target, myself, capacity):
    fields, cells_x, cells_y, lanes = state.shape
    owners, per_dev = target.shape
    f32 = jnp.float32
    hbm = pl.BlockSpec(memory_space=pltpu.HBM)
    vmem = pl.BlockSpec(memory_space=pltpu.VMEM)
    smem = pl.BlockSpec(memory_space=pltpu.SMEM)
    return pl.pallas_call(
        functools.partial(main_kernel, capacity),
        out_shape=(
            jax.ShapeDtypeStruct((fields, cells_x * cells_y // 8 + 2 * PAD, lanes), f32),
            jax.ShapeDtypeStruct((per_dev,), jnp.int32),
            jax.ShapeDtypeStruct((2, fields, cells_y, lanes), f32),
        ),
        in_specs=[smem, smem, hbm, hbm, hbm, hbm, hbm, hbm],
        out_specs=(vmem, smem, vmem),
        scratch_shapes=[
            pltpu.VMEM((fields, cells_x + 2, cells_y + 16, lanes), f32),
            pltpu.VMEM((fields, cells_x, cells_y, lanes), f32),
            pltpu.VMEM((fields, cells_x, cells_y, lanes), f32),
            pltpu.VMEM((cells_x, cells_y, lanes), f32),
            pltpu.VMEM((cells_x, cells_y, lanes), jnp.int32),
            pltpu.VMEM((2, fields, cells_y, lanes), f32),
            pltpu.VMEM((2 * lanes, lanes), jnp.bfloat16),
            pltpu.SMEM((8, per_dev), jnp.int32),
            pltpu.SMEM((owners,), jnp.int32),
            pltpu.SemaphoreType.DMA((cells_x // PLANES, 5)),
            pltpu.SemaphoreType.DMA((1,)),
        ],
        compiler_params=pltpu.CompilerParams(vmem_limit_bytes=36 * MIB),
        cost_estimate=pl.CostEstimate(flops=100_000_000, bytes_accessed=27_700_000, transcendentals=0),
        name="residual_pool",
    )(myself, in_hbm(coupling), in_hbm(target), in_hbm(state), in_hbm(adjoint), in_hbm(source), in_hbm(kappa), in_hbm(flags))


def pack_kernel(tile_rows, odd, slots, part, duals, inner, outer, out, stage, pe, wv, pv, sem):
    fields, cells_y, lanes = inner.shape
    rows = cells_y // 4
    per_dev = slots.shape[0]
    cells = part.shape[1] - 2 * PAD
    span = cells // per_dev
    kept = pe.shape[2] - 2 * PAD
    edge = edge_tiles(rows, span)
    pv[...] = pool_matrix(lanes)
    swapped = odd[0] != 0
    for f in range(fields):
        for y in range(0, cells_y, 8):
            here = pl.ds(y, 8)
            near, far = inner[f, here, :], outer[f, here, :]
            wv[0, f, here, :] = duals[0, f, here, :] * jnp.where(swapped, near, far)
            wv[1, f, here, :] = duals[1, f, here, :] * jnp.where(swapped, far, near)
    pooled = [pooled_rows(wv.at[i], pv[...]) for i in range(2)]
    for t in range(edge, per_dev - edge):
        values = tile_values(
            lambda f, d: part[f, pl.ds(PAD + span * t + d, 8), :], fields, span, tile_rows, lanes
        )
        send_tile(slots[t], t, values, stage, out, tile_rows, sem.at[0])
    for i, (at, start) in enumerate(((0, 0), (kept - rows, cells - kept))):
        for f in range(fields):
            pe[i, f, pl.ds(PAD, kept), :] = part[f, pl.ds(PAD + start, kept), :]
            here = pl.ds(at + PAD, rows)
            pe[i, f, here, :] = pe[i, f, here, :] + pooled[i][f * rows : (f + 1) * rows]
    for i, (tile, start) in enumerate(((0, 0), (per_dev - edge, kept - edge * span))):
        for k in range(edge):
            values = tile_values(
                lambda f, d: pe[i, f, pl.ds(PAD + start + span * k + d, 8), :], fields, span, tile_rows, lanes
            )
            send_tile(slots[tile + k], tile + k, values, stage, out, tile_rows, sem.at[0])
    await_tiles(0, per_dev, stage, out, tile_rows, sem.at[0])


def pack_part(odd, part, slots, duals, inner, outer, n_slots, tile_rows):
    fields, cells_y, lanes = inner.shape
    per_dev = slots.shape[0]
    span = (part.shape[1] - 2 * PAD) // per_dev
    kept = -(-edge_tiles(cells_y // 4, span) * span // 8) * 8
    f32 = jnp.float32
    vmem = pl.BlockSpec(memory_space=pltpu.VMEM)
    return pl.pallas_call(
        functools.partial(pack_kernel, tile_rows),
        out_shape=pltpu.HBM((n_slots * tile_rows, lanes), f32),
        in_specs=[pl.BlockSpec(memory_space=pltpu.SMEM)] * 2 + [vmem] * 4,
        out_specs=pl.BlockSpec(memory_space=pltpu.HBM),
        scratch_shapes=[
            pltpu.VMEM((per_dev * tile_rows, lanes), f32),
            pltpu.VMEM((2, fields, kept + 2 * PAD, lanes), f32),
            pltpu.VMEM((2, fields, cells_y, lanes), f32),
            pltpu.VMEM((2 * lanes, lanes), jnp.bfloat16),
            pltpu.SemaphoreType.DMA((1,)),
        ],
        compiler_params=pltpu.CompilerParams(vmem_limit_bytes=12 * MIB),
        cost_estimate=pl.CostEstimate(flops=1_000_000, bytes_accessed=3_500_000, transcendentals=0),
        name="edges_pack",
    )(odd, slots, part, duals, inner, outer)


def unpack_kernel(tile_rows, lookup, received, out, stage, built, sems):
    fields, per_dev, width = built.shape
    lanes = received.shape[1]
    span = width // lanes
    piece = per_dev // sems.shape[0]

    def leave(k):
        here = pl.ds(k * piece, piece)
        return pltpu.make_async_copy(built.at[:, here], out.at[:, here], sems.at[k])

    for g in range(per_dev // 8):
        buf = stage.at[g % stage.shape[0]]
        for s in range(8):
            base = pl.multiple_of(lookup[g * 8 + s] * tile_rows, 8)
            buf[pl.ds(s * (tile_rows + 1), tile_rows), :] = received[pl.ds(base, tile_rows), :]
        for f in range(fields):
            for j in range(span):
                rows = buf[pl.ds(f * span + j, 8, stride=tile_rows + 1), :]
                built[f, pl.ds(g * 8, 8), pl.ds(j * lanes, lanes)] = rows
        if (g + 1) * 8 % piece == 0:
            leave(g * 8 // piece).start()
    for k in range(sems.shape[0]):
        leave(k).wait()


def unpack_part(lookup, received, fields, per_dev, width, tile_rows):
    lanes = received.shape[1]
    return pl.pallas_call(
        functools.partial(unpack_kernel, tile_rows),
        out_shape=jax.ShapeDtypeStruct((fields, per_dev, width), jnp.float32),
        in_specs=[pl.BlockSpec(memory_space=pltpu.SMEM), pl.BlockSpec(memory_space=pltpu.VMEM)],
        out_specs=pl.BlockSpec(memory_space=pltpu.HBM),
        scratch_shapes=[
            pltpu.VMEM((4, 8 * (tile_rows + 1), lanes), jnp.float32),
            pltpu.VMEM((fields, per_dev, width), jnp.float32),
            pltpu.SemaphoreType.DMA((4,)),
        ],
        compiler_params=pltpu.CompilerParams(vmem_limit_bytes=8 * MIB),
        cost_estimate=pl.CostEstimate(flops=0, bytes_accessed=3_000_000, transcendentals=0),
        name="unpack",
    )(lookup, received)


def local(state, adjoint, source, kappa, cut_flags, coupling, target):
    state, adjoint, source, kappa, flags = (a[0] for a in (state, adjoint, source, kappa, cut_flags))
    fields, cells_x, cells_y, lanes = state.shape
    groups, bricks = lax.axis_size("grp"), lax.axis_size("brk")
    owners = groups * bricks
    per_dev = target.shape[1]
    capacity = per_dev // ((groups - 1) * bricks) + 1
    width = cells_x * cells_y * lanes // 8 // per_dev
    span = width // lanes
    tile_rows = -(-span * fields // 8) * 8
    myself = lax.axis_index(("grp", "brk"))

    odd = lax.rem(lax.axis_index("brk"), 2)
    one = [(i, i ^ 1) for i in range(bricks)]
    two = [(i, j) for i in range(1, bricks - 1) for j in (((i - 1) ^ 1) + 1,)]
    planes = state.reshape(fields * cells_x, cells_y, lanes)
    first = lax.slice(planes, (0, 0, 0), planes.shape, (cells_x, 1, 1))
    last = lax.slice(planes, (cells_x - 1, 0, 0), planes.shape, (cells_x, 1, 1))
    inner = lax.ppermute(jnp.where(odd == 0, last, first), "brk", one)
    outer = lax.ppermute(jnp.where(odd == 0, first, last), "brk", two)

    part, slots, duals = main_part(
        state, adjoint, source, kappa, flags, coupling, target, myself.reshape(1), capacity
    )
    outgoing = pack_part(odd.reshape(1), part, slots, duals, inner, outer, owners * capacity, tile_rows)
    outgoing = outgoing.reshape(owners, capacity * tile_rows, lanes)
    incoming = lax.all_to_all(outgoing, ("grp", "brk"), 0, 0, tiled=True)
    incoming = incoming.reshape(owners * capacity * tile_rows, lanes)

    slot_ids = myself * per_dev + jnp.arange(per_dev, dtype=jnp.int32)
    codes = jnp.arange(owners * per_dev, dtype=jnp.int32)
    hit = target.reshape(-1)[None, :] == slot_ids[:, None]
    origin = jnp.sum(jnp.where(hit, codes[None, :], 0), axis=1)
    sender = origin // per_dev
    before_it = jnp.logical_and(sender[:, None] == sender[None, :], origin[None, :] < origin[:, None])
    lookup = sender * capacity + jnp.sum(before_it.astype(jnp.int32), axis=1)
    out = unpack_part(lookup, incoming, fields, per_dev, width, tile_rows)
    return out.transpose(1, 0, 2)


def solution(mesh):
    placed = (
        P("grp", None, "brk", None, None),
        P("grp", None, "brk", None, None),
        P("grp", None, "brk", None, None),
        P("grp", "brk", None, None),
        P("grp", "brk", None, None),
        P(),
        P(),
    )
    return jax.shard_map(
        local, mesh=mesh, in_specs=placed, out_specs=P(("grp", "brk"), None, None), check_vma=False
    )
```

```python
import functools
import jax
import jax.numpy as jnp
from jax import lax
from jax.experimental import pallas as pl
from jax.experimental.pallas import tpu as pltpu
from jax.sharding import PartitionSpec as P

MIB = 1024 * 1024
PLANES = 4
PAD = 8


def in_hbm(x):
    return pltpu.with_memory_space_constraint(x, pltpu.HBM)


def weight_of(flags):
    return 1.0 - 0.5 * flags.astype(jnp.float32)


def pool_matrix(lanes):
    row = lax.broadcasted_iota(jnp.int32, (2 * lanes, lanes), 0)
    col = lax.broadcasted_iota(jnp.int32, (2 * lanes, lanes), 1)
    return jnp.where(row // 2 == col, 1.0, 0.0).astype(jnp.bfloat16)


def pooled_rows(fine_ref, matrix):
    fields, cells_y, _ = fine_ref.shape
    rows = cells_y // 4
    parts = [[fine_ref[f, pl.ds(k, rows, stride=4), :] for k in range(4)] for f in range(fields)]
    low = jnp.concatenate([p[0] + p[1] for p in parts], axis=0)
    high = jnp.concatenate([p[2] + p[3] for p in parts], axis=0)
    both = jnp.concatenate([low, high], axis=1)
    first = both.astype(jnp.bfloat16)
    rest = both - first.astype(jnp.float32)
    second = rest.astype(jnp.bfloat16)
    dot = functools.partial(jnp.dot, preferred_element_type=jnp.float32)
    return dot(first, matrix) + dot(second, matrix)


def tile_values(load, fields, span, tile_rows, lanes):
    sub = lax.broadcasted_iota(jnp.int32, (8, lanes), 0)
    values = []
    for v in range(tile_rows // 8):
        value = None
        for f in reversed(range(fields)):
            lo, hi = f * span - 8 * v, (f + 1) * span - 8 * v
            if hi <= 0 or lo >= 8:
                continue
            piece = load(f, -lo)
            value = piece if value is None else jnp.where(sub < hi, piece, value)
        values.append(value)
    return values


def send_tile(slot, at, values, stage, out, tile_rows, sem):
    for v, value in enumerate(values):
        stage[pl.ds(pl.multiple_of(at * tile_rows + 8 * v, 8), 8), :] = value
    here = pl.ds(pl.multiple_of(at * tile_rows, 8), tile_rows)
    there = pl.ds(pl.multiple_of(slot * tile_rows, 8), tile_rows)
    pltpu.make_async_copy(stage.at[here], out.at[there], sem).start()


def await_tiles(first, count, stage, out, tile_rows, sem):
    rows = count * tile_rows
    pltpu.make_async_copy(stage.at[pl.ds(first * tile_rows, rows)], out.at[pl.ds(0, rows)], sem).wait()


def edge_tiles(rows, span):
    return -(-rows // span)


def face_kernel(state, first, last, sems):
    cells_x = state.shape[1]
    one = pltpu.make_async_copy(state.at[:, 0], first, sems.at[0])
    two = pltpu.make_async_copy(state.at[:, cells_x - 1], last, sems.at[1])
    one.start()
    two.start()
    one.wait()
    two.wait()


def faces_of(state):
    fields, _, cells_y, lanes = state.shape
    face = jax.ShapeDtypeStruct((fields, cells_y, lanes), jnp.float32)
    vmem = pl.BlockSpec(memory_space=pltpu.VMEM)
    return pl.pallas_call(
        face_kernel,
        out_shape=(face, face),
        in_specs=[pl.BlockSpec(memory_space=pltpu.HBM)],
        out_specs=(vmem, vmem),
        scratch_shapes=[pltpu.SemaphoreType.DMA((2,))],
        compiler_params=pltpu.CompilerParams(vmem_limit_bytes=2 * MIB),
        cost_estimate=pl.CostEstimate(flops=0, bytes_accessed=650_000, transcendentals=0),
        name="faces",
    )(in_hbm(state))


def main_kernel(
    capacity, myself, coupling, target, state, adjoint, source, kappa, flags,
    out, slots, duals, sv, av, bv, kv, fv, wv, pv, tv, seen, sems, tsem,
):
    fields, cells_x, cells_y, lanes = adjoint.shape
    steps = cells_x // PLANES
    rows = cells_y // 4
    owners, per_dev = target.shape

    def copy(step, i):
        at = pl.ds(PLANES * step, PLANES)
        if i == 0:
            landing = sv.at[:, pl.ds(PLANES * step + 1, PLANES), pl.ds(8, cells_y)]
            return pltpu.make_async_copy(state.at[:, at], landing, sems.at[step, 0])
        if i > 2:
            src, dst = ((kappa, kv), (flags, fv))[i - 3]
            return pltpu.make_async_copy(src.at[at], dst.at[at], sems.at[step, i])
        src, dst = ((adjoint, av), (source, bv))[i - 1]
        return pltpu.make_async_copy(src.at[:, at], dst.at[:, at], sems.at[step, i])

    def start(step):
        copy(step + 1, 0).start()
        for i in range(1, 5):
            copy(step, i).start()

    me = myself[0]
    row8 = pl.multiple_of(lax.shift_left(lax.shift_right_logical(me, 3), 3), 8)
    table = pltpu.make_async_copy(target.at[pl.ds(row8, 8)], tv, tsem.at[0])
    table.start()
    copy(0, 0).start()
    for step in range(steps - 1):
        start(step)
    for i in range(1, 5):
        copy(steps - 1, i).start()
    zero = jnp.zeros((8, lanes), jnp.float32)
    pv[...] = pool_matrix(lanes)

    def clear(x, carry):
        for f in range(fields):
            sv[f, x, pl.ds(0, 8), :] = zero
            sv[f, x, pl.ds(cells_y + 8, 8), :] = zero
        return carry

    lax.fori_loop(0, cells_x + 2, clear, 0)
    for f in range(fields):
        for y in range(0, cells_y, 8):
            sv[f, 0, pl.ds(y + 8, 8), :] = zero
            sv[f, cells_x + 1, pl.ds(y + 8, 8), :] = zero

    for i in range(owners):
        seen[i] = 0
    table.wait()
    mine = lax.bitwise_and(me, 7)

    def rank(t, carry):
        owner = lax.shift_right_logical(tv[mine, t], per_dev.bit_length() - 1)
        count = seen[owner]
        slots[t] = owner * capacity + count
        seen[owner] = count + 1
        return carry

    lax.fori_loop(0, per_dev, rank, 0, unroll=8)

    coef = [[coupling[f, h] for h in range(fields)] for f in range(fields)]
    lane = lax.broadcasted_iota(jnp.int32, (8, lanes), 1)
    inner_lo = lane != 0
    inner_hi = lane != lanes - 1

    def pool(half, at):
        pooled = pooled_rows(wv.at[half], pv[...])
        for f in range(fields):
            out[f, pl.ds(pl.multiple_of(at + PAD, 8), rows), :] = pooled[f * rows : (f + 1) * rows]

    copy(0, 0).wait()
    def step_body(step, carry):
        @pl.when(step + 1 < steps)
        def _():
            copy(step + 1, 0).wait()

        for i in range(1, 5):
            copy(step, i).wait()

        for half in range(PLANES // 2):
            coarse = step * (PLANES // 2) + half
            pool(1 - half % 2, jnp.maximum(coarse - 1, 0) * rows)
            for y in range(0, cells_y, 8):
                total = [None] * fields
                for p in range(2):
                    x = 2 * coarse + p
                    kap = kv[x, pl.ds(y, 8), :]
                    wgt = weight_of(fv[x, pl.ds(y, 8), :])
                    mid = [sv[f, x + 1, pl.ds(y + 8, 8), :] for f in range(fields)]
                    for f in range(fields):
                        near = sv[f, x, pl.ds(y + 8, 8), :] + sv[f, x + 2, pl.ds(y + 8, 8), :]
                        near = near + sv[f, x + 1, pl.ds(y + 7, 8), :] + sv[f, x + 1, pl.ds(y + 9, 8), :]
                        near = near + jnp.where(inner_lo, pltpu.roll(mid[f], 1, 1), 0.0)
                        near = near + jnp.where(inner_hi, pltpu.roll(mid[f], lanes - 1, 1), 0.0)
                        applied = (kap + (coef[f][f] + 6.0)) * mid[f]
                        for h in range(fields):
                            if h != f:
                                applied = applied + coef[f][h] * mid[h]
                        residual = bv[f, x, pl.ds(y, 8), :] - applied + near
                        term = wgt * av[f, x, pl.ds(y, 8), :] * residual
                        total[f] = term if p == 0 else total[f] + term
                for f in range(fields):
                    wv[half % 2, f, pl.ds(y, 8), :] = total[f]
        return carry

    lax.fori_loop(0, steps, step_body, 0)
    pool(1, (cells_x // 2 - 1) * rows)
    for i, x in enumerate((0, cells_x - 1)):
        for y in range(0, cells_y, 8):
            wgt = weight_of(fv[x, pl.ds(y, 8), :])
            for f in range(fields):
                duals[i, f, pl.ds(y, 8), :] = wgt * av[f, x, pl.ds(y, 8), :]

def main_part(state, adjoint, source, kappa, flags, coupling, target, myself, capacity):
    fields, cells_x, cells_y, lanes = state.shape
    owners, per_dev = target.shape
    f32 = jnp.float32
    hbm = pl.BlockSpec(memory_space=pltpu.HBM)
    vmem = pl.BlockSpec(memory_space=pltpu.VMEM)
    smem = pl.BlockSpec(memory_space=pltpu.SMEM)
    return pl.pallas_call(
        functools.partial(main_kernel, capacity),
        out_shape=(
            jax.ShapeDtypeStruct((fields, cells_x * cells_y // 8 + 2 * PAD, lanes), f32),
            jax.ShapeDtypeStruct((per_dev,), jnp.int32),
            jax.ShapeDtypeStruct((2, fields, cells_y, lanes), f32),
        ),
        in_specs=[smem, smem, hbm, hbm, hbm, hbm, hbm, hbm],
        out_specs=(vmem, smem, vmem),
        scratch_shapes=[
            pltpu.VMEM((fields, cells_x + 2, cells_y + 16, lanes), f32),
            pltpu.VMEM((fields, cells_x, cells_y, lanes), f32),
            pltpu.VMEM((fields, cells_x, cells_y, lanes), f32),
            pltpu.VMEM((cells_x, cells_y, lanes), f32),
            pltpu.VMEM((cells_x, cells_y, lanes), jnp.int32),
            pltpu.VMEM((2, fields, cells_y, lanes), f32),
            pltpu.VMEM((2 * lanes, lanes), jnp.bfloat16),
            pltpu.SMEM((8, per_dev), jnp.int32),
            pltpu.SMEM((owners,), jnp.int32),
            pltpu.SemaphoreType.DMA((cells_x // PLANES, 5)),
            pltpu.SemaphoreType.DMA((1,)),
        ],
        compiler_params=pltpu.CompilerParams(vmem_limit_bytes=36 * MIB),
        cost_estimate=pl.CostEstimate(flops=100_000_000, bytes_accessed=27_700_000, transcendentals=0),
        name="residual_pool",
    )(myself, in_hbm(coupling), in_hbm(target), in_hbm(state), in_hbm(adjoint), in_hbm(source), in_hbm(kappa), in_hbm(flags))


def pack_kernel(tile_rows, odd, slots, part, duals, inner, outer, out, stage, pe, wv, pv, sem):
    fields, cells_y, lanes = inner.shape
    rows = cells_y // 4
    per_dev = slots.shape[0]
    cells = part.shape[1] - 2 * PAD
    span = cells // per_dev
    kept = pe.shape[2] - 2 * PAD
    edge = edge_tiles(rows, span)
    pv[...] = pool_matrix(lanes)
    swapped = odd[0] != 0
    for f in range(fields):
        for y in range(0, cells_y, 8):
            here = pl.ds(y, 8)
            near, far = inner[f, here, :], outer[f, here, :]
            wv[0, f, here, :] = duals[0, f, here, :] * jnp.where(swapped, near, far)
            wv[1, f, here, :] = duals[1, f, here, :] * jnp.where(swapped, far, near)
    pooled = [pooled_rows(wv.at[i], pv[...]) for i in range(2)]
    for t in range(edge, per_dev - edge):
        values = tile_values(
            lambda f, d: part[f, pl.ds(PAD + span * t + d, 8), :], fields, span, tile_rows, lanes
        )
        send_tile(slots[t], t, values, stage, out, tile_rows, sem.at[0])
    for i, (at, start) in enumerate(((0, 0), (kept - rows, cells - kept))):
        for f in range(fields):
            pe[i, f, pl.ds(PAD, kept), :] = part[f, pl.ds(PAD + start, kept), :]
            here = pl.ds(at + PAD, rows)
            pe[i, f, here, :] = pe[i, f, here, :] + pooled[i][f * rows : (f + 1) * rows]
    for i, (tile, start) in enumerate(((0, 0), (per_dev - edge, kept - edge * span))):
        for k in range(edge):
            values = tile_values(
                lambda f, d: pe[i, f, pl.ds(PAD + start + span * k + d, 8), :], fields, span, tile_rows, lanes
            )
            send_tile(slots[tile + k], tile + k, values, stage, out, tile_rows, sem.at[0])
    await_tiles(0, per_dev, stage, out, tile_rows, sem.at[0])


def pack_part(odd, part, slots, duals, inner, outer, n_slots, tile_rows):
    fields, cells_y, lanes = inner.shape
    per_dev = slots.shape[0]
    span = (part.shape[1] - 2 * PAD) // per_dev
    kept = -(-edge_tiles(cells_y // 4, span) * span // 8) * 8
    f32 = jnp.float32
    vmem = pl.BlockSpec(memory_space=pltpu.VMEM)
    return pl.pallas_call(
        functools.partial(pack_kernel, tile_rows),
        out_shape=pltpu.HBM((n_slots * tile_rows, lanes), f32),
        in_specs=[pl.BlockSpec(memory_space=pltpu.SMEM)] * 2 + [vmem] * 4,
        out_specs=pl.BlockSpec(memory_space=pltpu.HBM),
        scratch_shapes=[
            pltpu.VMEM((per_dev * tile_rows, lanes), f32),
            pltpu.VMEM((2, fields, kept + 2 * PAD, lanes), f32),
            pltpu.VMEM((2, fields, cells_y, lanes), f32),
            pltpu.VMEM((2 * lanes, lanes), jnp.bfloat16),
            pltpu.SemaphoreType.DMA((1,)),
        ],
        compiler_params=pltpu.CompilerParams(vmem_limit_bytes=12 * MIB),
        cost_estimate=pl.CostEstimate(flops=1_000_000, bytes_accessed=3_500_000, transcendentals=0),
        name="edges_pack",
    )(odd, slots, part, duals, inner, outer)


def unpack_kernel(tile_rows, lookup, received, out, stage, built, sems):
    fields, per_dev, width = built.shape
    lanes = received.shape[1]
    span = width // lanes
    piece = per_dev // sems.shape[0]

    def leave(k):
        here = pl.ds(k * piece, piece)
        return pltpu.make_async_copy(built.at[:, here], out.at[:, here], sems.at[k])

    for g in range(per_dev // 8):
        buf = stage.at[g % stage.shape[0]]
        for s in range(8):
            base = pl.multiple_of(lookup[g * 8 + s] * tile_rows, 8)
            buf[pl.ds(s * (tile_rows + 1), tile_rows), :] = received[pl.ds(base, tile_rows), :]
        for f in range(fields):
            for j in range(span):
                rows = buf[pl.ds(f * span + j, 8, stride=tile_rows + 1), :]
                built[f, pl.ds(g * 8, 8), pl.ds(j * lanes, lanes)] = rows
        if (g + 1) * 8 % piece == 0:
            leave(g * 8 // piece).start()
    for k in range(sems.shape[0]):
        leave(k).wait()


def unpack_part(lookup, received, fields, per_dev, width, tile_rows):
    lanes = received.shape[1]
    return pl.pallas_call(
        functools.partial(unpack_kernel, tile_rows),
        out_shape=jax.ShapeDtypeStruct((fields, per_dev, width), jnp.float32),
        in_specs=[pl.BlockSpec(memory_space=pltpu.SMEM), pl.BlockSpec(memory_space=pltpu.VMEM)],
        out_specs=pl.BlockSpec(memory_space=pltpu.HBM),
        scratch_shapes=[
            pltpu.VMEM((4, 8 * (tile_rows + 1), lanes), jnp.float32),
            pltpu.VMEM((fields, per_dev, width), jnp.float32),
            pltpu.SemaphoreType.DMA((4,)),
        ],
        compiler_params=pltpu.CompilerParams(vmem_limit_bytes=8 * MIB),
        cost_estimate=pl.CostEstimate(flops=0, bytes_accessed=3_000_000, transcendentals=0),
        name="unpack",
    )(lookup, received)


def local(state, adjoint, source, kappa, cut_flags, coupling, target):
    state, adjoint, source, kappa, flags = (a[0] for a in (state, adjoint, source, kappa, cut_flags))
    fields, cells_x, cells_y, lanes = state.shape
    groups, bricks = lax.axis_size("grp"), lax.axis_size("brk")
    owners = groups * bricks
    per_dev = target.shape[1]
    capacity = per_dev // ((groups - 1) * bricks) + 1
    width = cells_x * cells_y * lanes // 8 // per_dev
    span = width // lanes
    tile_rows = -(-span * fields // 8) * 8
    myself = lax.axis_index(("grp", "brk"))

    odd = lax.rem(lax.axis_index("brk"), 2)
    one = [(i, i ^ 1) for i in range(bricks)]
    two = [(i, j) for i in range(1, bricks - 1) for j in (((i - 1) ^ 1) + 1,)]
    planes = state.reshape(fields * cells_x, cells_y, lanes)
    first = lax.slice(planes, (0, 0, 0), planes.shape, (cells_x, 1, 1))
    last = lax.slice(planes, (cells_x - 1, 0, 0), planes.shape, (cells_x, 1, 1))
    inner = lax.ppermute(jnp.where(odd == 0, last, first), "brk", one)
    outer = lax.ppermute(jnp.where(odd == 0, first, last), "brk", two)

    part, slots, duals = main_part(
        state, adjoint, source, kappa, flags, coupling, target, myself.reshape(1), capacity
    )
    outgoing = pack_part(odd.reshape(1), part, slots, duals, inner, outer, owners * capacity, tile_rows)
    outgoing = outgoing.reshape(owners, capacity * tile_rows, lanes)
    incoming = lax.all_to_all(outgoing, ("grp", "brk"), 0, 0, tiled=True)
    incoming = incoming.reshape(owners * capacity * tile_rows, lanes)

    slot_ids = myself * per_dev + jnp.arange(per_dev, dtype=jnp.int32)
    codes = jnp.arange(owners * per_dev, dtype=jnp.int32)
    hit = target.reshape(-1)[None, :] == slot_ids[:, None]
    origin = jnp.sum(jnp.where(hit, codes[None, :], 0), axis=1)
    sender = origin // per_dev
    before_it = jnp.logical_and(sender[:, None] == sender[None, :], origin[None, :] < origin[:, None])
    lookup = sender * capacity + jnp.sum(before_it.astype(jnp.int32), axis=1)
    out = unpack_part(lookup, incoming, fields, per_dev, width, tile_rows)
    return out.transpose(1, 0, 2)


def solution(mesh):
    placed = (
        P("grp", None, "brk", None, None),
        P("grp", None, "brk", None, None),
        P("grp", None, "brk", None, None),
        P("grp", "brk", None, None),
        P("grp", "brk", None, None),
        P(),
        P(),
    )
    return jax.shard_map(
        local, mesh=mesh, in_specs=placed, out_specs=P(("grp", "brk"), None, None), check_vma=False
    )
```

```python
import functools
import jax
import jax.numpy as jnp
from jax import lax
from jax.experimental import pallas as pl
from jax.experimental.pallas import tpu as pltpu
from jax.sharding import PartitionSpec as P

MIB = 1024 * 1024
PLANES = 4
PAD = 8


def in_hbm(x):
    return pltpu.with_memory_space_constraint(x, pltpu.HBM)


def weight_of(flags):
    return 1.0 - 0.5 * flags.astype(jnp.float32)


def pool_matrix(lanes):
    row = lax.broadcasted_iota(jnp.int32, (2 * lanes, lanes), 0)
    col = lax.broadcasted_iota(jnp.int32, (2 * lanes, lanes), 1)
    return jnp.where(row // 2 == col, 1.0, 0.0).astype(jnp.bfloat16)


def pooled_rows(fine_ref, matrix):
    fields, cells_y, _ = fine_ref.shape
    rows = cells_y // 4
    parts = [[fine_ref[f, pl.ds(k, rows, stride=4), :] for k in range(4)] for f in range(fields)]
    low = jnp.concatenate([p[0] + p[1] for p in parts], axis=0)
    high = jnp.concatenate([p[2] + p[3] for p in parts], axis=0)
    both = jnp.concatenate([low, high], axis=1)
    first = both.astype(jnp.bfloat16)
    rest = both - first.astype(jnp.float32)
    second = rest.astype(jnp.bfloat16)
    dot = functools.partial(jnp.dot, preferred_element_type=jnp.float32)
    return dot(first, matrix) + dot(second, matrix)


def tile_values(load, fields, span, tile_rows, lanes):
    sub = lax.broadcasted_iota(jnp.int32, (8, lanes), 0)
    values = []
    for v in range(tile_rows // 8):
        value = None
        for f in reversed(range(fields)):
            lo, hi = f * span - 8 * v, (f + 1) * span - 8 * v
            if hi <= 0 or lo >= 8:
                continue
            piece = load(f, -lo)
            value = piece if value is None else jnp.where(sub < hi, piece, value)
        values.append(value)
    return values


def send_tile(slot, at, values, stage, out, tile_rows, sem):
    for v, value in enumerate(values):
        stage[pl.ds(pl.multiple_of(at * tile_rows + 8 * v, 8), 8), :] = value
    here = pl.ds(pl.multiple_of(at * tile_rows, 8), tile_rows)
    there = pl.ds(pl.multiple_of(slot * tile_rows, 8), tile_rows)
    pltpu.make_async_copy(stage.at[here], out.at[there], sem).start()


def await_tiles(first, count, stage, out, tile_rows, sem):
    rows = count * tile_rows
    pltpu.make_async_copy(stage.at[pl.ds(first * tile_rows, rows)], out.at[pl.ds(0, rows)], sem).wait()


def edge_tiles(rows, span):
    return -(-rows // span)


def face_kernel(state, first, last, sems):
    cells_x = state.shape[1]
    one = pltpu.make_async_copy(state.at[:, 0], first, sems.at[0])
    two = pltpu.make_async_copy(state.at[:, cells_x - 1], last, sems.at[1])
    one.start()
    two.start()
    one.wait()
    two.wait()


def faces_of(state):
    fields, _, cells_y, lanes = state.shape
    face = jax.ShapeDtypeStruct((fields, cells_y, lanes), jnp.float32)
    vmem = pl.BlockSpec(memory_space=pltpu.VMEM)
    return pl.pallas_call(
        face_kernel,
        out_shape=(face, face),
        in_specs=[pl.BlockSpec(memory_space=pltpu.HBM)],
        out_specs=(vmem, vmem),
        scratch_shapes=[pltpu.SemaphoreType.DMA((2,))],
        compiler_params=pltpu.CompilerParams(vmem_limit_bytes=2 * MIB),
        cost_estimate=pl.CostEstimate(flops=0, bytes_accessed=650_000, transcendentals=0),
        name="faces",
    )(in_hbm(state))


def main_kernel(
    capacity, myself, coupling, target, state, adjoint, source, kappa, flags,
    out, slots, duals, sv, av, bv, kv, fv, wv, pv, tv, seen, sems, tsem,
):
    fields, cells_x, cells_y, lanes = adjoint.shape
    steps = cells_x // PLANES
    rows = cells_y // 4
    owners, per_dev = target.shape

    def copy(step, i):
        at = pl.ds(PLANES * step, PLANES)
        if i == 0:
            landing = sv.at[:, pl.ds(PLANES * step + 1, PLANES), pl.ds(8, cells_y)]
            return pltpu.make_async_copy(state.at[:, at], landing, sems.at[step, 0])
        if i > 2:
            src, dst = ((kappa, kv), (flags, fv))[i - 3]
            return pltpu.make_async_copy(src.at[at], dst.at[at], sems.at[step, i])
        src, dst = ((adjoint, av), (source, bv))[i - 1]
        return pltpu.make_async_copy(src.at[:, at], dst.at[:, at], sems.at[step, i])

    def start(step):
        copy(step + 1, 0).start()
        for i in range(1, 5):
            copy(step, i).start()

    me = myself[0]
    row8 = pl.multiple_of(lax.shift_left(lax.shift_right_logical(me, 3), 3), 8)
    table = pltpu.make_async_copy(target.at[pl.ds(row8, 8)], tv, tsem.at[0])
    table.start()
    copy(0, 0).start()
    for step in range(steps - 1):
        start(step)
    for i in range(1, 5):
        copy(steps - 1, i).start()
    zero = jnp.zeros((8, lanes), jnp.float32)
    pv[...] = pool_matrix(lanes)

    def clear(x, carry):
        for f in range(fields):
            sv[f, x, pl.ds(0, 8), :] = zero
            sv[f, x, pl.ds(cells_y + 8, 8), :] = zero
        return carry

    lax.fori_loop(0, cells_x + 2, clear, 0)
    for f in range(fields):
        for y in range(0, cells_y, 8):
            sv[f, 0, pl.ds(y + 8, 8), :] = zero
            sv[f, cells_x + 1, pl.ds(y + 8, 8), :] = zero

    for i in range(owners):
        seen[i] = 0
    table.wait()
    mine = lax.bitwise_and(me, 7)

    def rank(t, carry):
        owner = lax.shift_right_logical(tv[mine, t], per_dev.bit_length() - 1)
        count = seen[owner]
        slots[t] = owner * capacity + count
        seen[owner] = count + 1
        return carry

    lax.fori_loop(0, per_dev, rank, 0, unroll=8)

    coef = [[coupling[f, h] for h in range(fields)] for f in range(fields)]
    lane = lax.broadcasted_iota(jnp.int32, (8, lanes), 1)
    inner_lo = lane != 0
    inner_hi = lane != lanes - 1

    def pool(half, at):
        pooled = pooled_rows(wv.at[half], pv[...])
        for f in range(fields):
            out[f, pl.ds(pl.multiple_of(at + PAD, 8), rows), :] = pooled[f * rows : (f + 1) * rows]

    copy(0, 0).wait()
    def step_body(step, carry):
        @pl.when(step + 1 < steps)
        def _():
            copy(step + 1, 0).wait()

        for i in range(1, 5):
            copy(step, i).wait()

        for half in range(PLANES // 2):
            coarse = step * (PLANES // 2) + half
            pool(1 - half % 2, jnp.maximum(coarse - 1, 0) * rows)
            for y in range(0, cells_y, 8):
                total = [None] * fields
                for p in range(2):
                    x = 2 * coarse + p
                    kap = kv[x, pl.ds(y, 8), :]
                    wgt = weight_of(fv[x, pl.ds(y, 8), :])
                    mid = [sv[f, x + 1, pl.ds(y + 8, 8), :] for f in range(fields)]
                    for f in range(fields):
                        near = sv[f, x, pl.ds(y + 8, 8), :] + sv[f, x + 2, pl.ds(y + 8, 8), :]
                        near = near + sv[f, x + 1, pl.ds(y + 7, 8), :] + sv[f, x + 1, pl.ds(y + 9, 8), :]
                        near = near + jnp.where(inner_lo, pltpu.roll(mid[f], 1, 1), 0.0)
                        near = near + jnp.where(inner_hi, pltpu.roll(mid[f], lanes - 1, 1), 0.0)
                        applied = (kap + (coef[f][f] + 6.0)) * mid[f]
                        for h in range(fields):
                            if h != f:
                                applied = applied + coef[f][h] * mid[h]
                        residual = bv[f, x, pl.ds(y, 8), :] - applied + near
                        term = wgt * av[f, x, pl.ds(y, 8), :] * residual
                        total[f] = term if p == 0 else total[f] + term
                for f in range(fields):
                    wv[half % 2, f, pl.ds(y, 8), :] = total[f]
        return carry

    lax.fori_loop(0, steps, step_body, 0)
    pool(1, (cells_x // 2 - 1) * rows)
    for i, x in enumerate((0, cells_x - 1)):
        for y in range(0, cells_y, 8):
            wgt = weight_of(fv[x, pl.ds(y, 8), :])
            for f in range(fields):
                duals[i, f, pl.ds(y, 8), :] = wgt * av[f, x, pl.ds(y, 8), :]

def main_part(state, adjoint, source, kappa, flags, coupling, target, myself, capacity):
    fields, cells_x, cells_y, lanes = state.shape
    owners, per_dev = target.shape
    f32 = jnp.float32
    hbm = pl.BlockSpec(memory_space=pltpu.HBM)
    vmem = pl.BlockSpec(memory_space=pltpu.VMEM)
    smem = pl.BlockSpec(memory_space=pltpu.SMEM)
    return pl.pallas_call(
        functools.partial(main_kernel, capacity),
        out_shape=(
            jax.ShapeDtypeStruct((fields, cells_x * cells_y // 8 + 2 * PAD, lanes), f32),
            jax.ShapeDtypeStruct((per_dev,), jnp.int32),
            jax.ShapeDtypeStruct((2, fields, cells_y, lanes), f32),
        ),
        in_specs=[smem, smem, hbm, hbm, hbm, hbm, hbm, hbm],
        out_specs=(vmem, smem, vmem),
        scratch_shapes=[
            pltpu.VMEM((fields, cells_x + 2, cells_y + 16, lanes), f32),
            pltpu.VMEM((fields, cells_x, cells_y, lanes), f32),
            pltpu.VMEM((fields, cells_x, cells_y, lanes), f32),
            pltpu.VMEM((cells_x, cells_y, lanes), f32),
            pltpu.VMEM((cells_x, cells_y, lanes), jnp.int32),
            pltpu.VMEM((2, fields, cells_y, lanes), f32),
            pltpu.VMEM((2 * lanes, lanes), jnp.bfloat16),
            pltpu.SMEM((8, per_dev), jnp.int32),
            pltpu.SMEM((owners,), jnp.int32),
            pltpu.SemaphoreType.DMA((cells_x // PLANES, 5)),
            pltpu.SemaphoreType.DMA((1,)),
        ],
        compiler_params=pltpu.CompilerParams(vmem_limit_bytes=36 * MIB),
        cost_estimate=pl.CostEstimate(flops=100_000_000, bytes_accessed=27_700_000, transcendentals=0),
        name="residual_pool",
    )(myself, in_hbm(coupling), in_hbm(target), in_hbm(state), in_hbm(adjoint), in_hbm(source), in_hbm(kappa), in_hbm(flags))


def pack_kernel(tile_rows, odd, slots, part, duals, inner, outer, out, stage, pe, wv, pv, sem):
    fields, cells_y, lanes = inner.shape
    rows = cells_y // 4
    per_dev = slots.shape[0]
    cells = part.shape[1] - 2 * PAD
    span = cells // per_dev
    kept = pe.shape[2] - 2 * PAD
    edge = edge_tiles(rows, span)
    for t in range(edge, per_dev - edge):
        values = tile_values(
            lambda f, d: part[f, pl.ds(PAD + span * t + d, 8), :], fields, span, tile_rows, lanes
        )
        send_tile(slots[t], t, values, stage, out, tile_rows, sem.at[0])
    pv[...] = pool_matrix(lanes)
    swapped = odd[0] != 0
    for f in range(fields):
        for y in range(0, cells_y, 8):
            here = pl.ds(y, 8)
            near, far = inner[f, here, :], outer[f, here, :]
            wv[0, f, here, :] = duals[0, f, here, :] * jnp.where(swapped, near, far)
            wv[1, f, here, :] = duals[1, f, here, :] * jnp.where(swapped, far, near)
    pooled = [pooled_rows(wv.at[i], pv[...]) for i in range(2)]
    for i, (at, start) in enumerate(((0, 0), (kept - rows, cells - kept))):
        for f in range(fields):
            pe[i, f, pl.ds(PAD, kept), :] = part[f, pl.ds(PAD + start, kept), :]
            here = pl.ds(at + PAD, rows)
            pe[i, f, here, :] = pe[i, f, here, :] + pooled[i][f * rows : (f + 1) * rows]
    for i, (tile, start) in enumerate(((0, 0), (per_dev - edge, kept - edge * span))):
        for k in range(edge):
            values = tile_values(
                lambda f, d: pe[i, f, pl.ds(PAD + start + span * k + d, 8), :], fields, span, tile_rows, lanes
            )
            send_tile(slots[tile + k], tile + k, values, stage, out, tile_rows, sem.at[0])
    await_tiles(0, per_dev, stage, out, tile_rows, sem.at[0])


def pack_part(odd, part, slots, duals, inner, outer, n_slots, tile_rows):
    fields, cells_y, lanes = inner.shape
    per_dev = slots.shape[0]
    span = (part.shape[1] - 2 * PAD) // per_dev
    kept = -(-edge_tiles(cells_y // 4, span) * span // 8) * 8
    f32 = jnp.float32
    vmem = pl.BlockSpec(memory_space=pltpu.VMEM)
    return pl.pallas_call(
        functools.partial(pack_kernel, tile_rows),
        out_shape=pltpu.HBM((n_slots * tile_rows, lanes), f32),
        in_specs=[pl.BlockSpec(memory_space=pltpu.SMEM)] * 2 + [vmem] * 4,
        out_specs=pl.BlockSpec(memory_space=pltpu.HBM),
        scratch_shapes=[
            pltpu.VMEM((per_dev * tile_rows, lanes), f32),
            pltpu.VMEM((2, fields, kept + 2 * PAD, lanes), f32),
            pltpu.VMEM((2, fields, cells_y, lanes), f32),
            pltpu.VMEM((2 * lanes, lanes), jnp.bfloat16),
            pltpu.SemaphoreType.DMA((1,)),
        ],
        compiler_params=pltpu.CompilerParams(vmem_limit_bytes=12 * MIB),
        cost_estimate=pl.CostEstimate(flops=1_000_000, bytes_accessed=3_500_000, transcendentals=0),
        name="edges_pack",
    )(odd, slots, part, duals, inner, outer)


def unpack_kernel(tile_rows, lookup, received, out, stage, built, sems):
    fields, per_dev, width = built.shape
    lanes = received.shape[1]
    span = width // lanes
    piece = per_dev // sems.shape[0]

    def leave(k):
        here = pl.ds(k * piece, piece)
        return pltpu.make_async_copy(built.at[:, here], out.at[:, here], sems.at[k])

    for g in range(per_dev // 8):
        buf = stage.at[g % stage.shape[0]]
        for s in range(8):
            base = pl.multiple_of(lookup[g * 8 + s] * tile_rows, 8)
            buf[pl.ds(s * (tile_rows + 1), tile_rows), :] = received[pl.ds(base, tile_rows), :]
        for f in range(fields):
            for j in range(span):
                rows = buf[pl.ds(f * span + j, 8, stride=tile_rows + 1), :]
                built[f, pl.ds(g * 8, 8), pl.ds(j * lanes, lanes)] = rows
        if (g + 1) * 8 % piece == 0:
            leave(g * 8 // piece).start()
    for k in range(sems.shape[0]):
        leave(k).wait()


def unpack_part(lookup, received, fields, per_dev, width, tile_rows):
    lanes = received.shape[1]
    return pl.pallas_call(
        functools.partial(unpack_kernel, tile_rows),
        out_shape=jax.ShapeDtypeStruct((fields, per_dev, width), jnp.float32),
        in_specs=[pl.BlockSpec(memory_space=pltpu.SMEM), pl.BlockSpec(memory_space=pltpu.VMEM)],
        out_specs=pl.BlockSpec(memory_space=pltpu.HBM),
        scratch_shapes=[
            pltpu.VMEM((4, 8 * (tile_rows + 1), lanes), jnp.float32),
            pltpu.VMEM((fields, per_dev, width), jnp.float32),
            pltpu.SemaphoreType.DMA((4,)),
        ],
        compiler_params=pltpu.CompilerParams(vmem_limit_bytes=8 * MIB),
        cost_estimate=pl.CostEstimate(flops=0, bytes_accessed=3_000_000, transcendentals=0),
        name="unpack",
    )(lookup, received)


def local(state, adjoint, source, kappa, cut_flags, coupling, target):
    state, adjoint, source, kappa, flags = (a[0] for a in (state, adjoint, source, kappa, cut_flags))
    fields, cells_x, cells_y, lanes = state.shape
    groups, bricks = lax.axis_size("grp"), lax.axis_size("brk")
    owners = groups * bricks
    per_dev = target.shape[1]
    capacity = per_dev // ((groups - 1) * bricks) + 1
    width = cells_x * cells_y * lanes // 8 // per_dev
    span = width // lanes
    tile_rows = -(-span * fields // 8) * 8
    myself = lax.axis_index(("grp", "brk"))

    odd = lax.rem(lax.axis_index("brk"), 2)
    one = [(i, i ^ 1) for i in range(bricks)]
    two = [(i, j) for i in range(1, bricks - 1) for j in (((i - 1) ^ 1) + 1,)]
    planes = state.reshape(fields * cells_x, cells_y, lanes)
    first = lax.slice(planes, (0, 0, 0), planes.shape, (cells_x, 1, 1))
    last = lax.slice(planes, (cells_x - 1, 0, 0), planes.shape, (cells_x, 1, 1))
    inner = lax.ppermute(jnp.where(odd == 0, last, first), "brk", one)
    outer = lax.ppermute(jnp.where(odd == 0, first, last), "brk", two)

    part, slots, duals = main_part(
        state, adjoint, source, kappa, flags, coupling, target, myself.reshape(1), capacity
    )
    outgoing = pack_part(odd.reshape(1), part, slots, duals, inner, outer, owners * capacity, tile_rows)
    outgoing = outgoing.reshape(owners, capacity * tile_rows, lanes)
    incoming = lax.all_to_all(outgoing, ("grp", "brk"), 0, 0, tiled=True)
    incoming = incoming.reshape(owners * capacity * tile_rows, lanes)

    slot_ids = myself * per_dev + jnp.arange(per_dev, dtype=jnp.int32)
    codes = jnp.arange(owners * per_dev, dtype=jnp.int32)
    hit = target.reshape(-1)[None, :] == slot_ids[:, None]
    origin = jnp.sum(jnp.where(hit, codes[None, :], 0), axis=1)
    sender = origin // per_dev
    before_it = jnp.logical_and(sender[:, None] == sender[None, :], origin[None, :] < origin[:, None])
    lookup = sender * capacity + jnp.sum(before_it.astype(jnp.int32), axis=1)
    out = unpack_part(lookup, incoming, fields, per_dev, width, tile_rows)
    return out.transpose(1, 0, 2)


def solution(mesh):
    placed = (
        P("grp", None, "brk", None, None),
        P("grp", None, "brk", None, None),
        P("grp", None, "brk", None, None),
        P("grp", "brk", None, None),
        P("grp", "brk", None, None),
        P(),
        P(),
    )
    return jax.shard_map(
        local, mesh=mesh, in_specs=placed, out_specs=P(("grp", "brk"), None, None), check_vma=False
    )
```

```python
import functools
import jax
import jax.numpy as jnp
from jax import lax
from jax.experimental import pallas as pl
from jax.experimental.pallas import tpu as pltpu
from jax.sharding import PartitionSpec as P

MIB = 1024 * 1024
PLANES = 4
PAD = 8


def in_hbm(x):
    return pltpu.with_memory_space_constraint(x, pltpu.HBM)


def weight_of(flags):
    return 1.0 - 0.5 * flags.astype(jnp.float32)


def pool_matrix(lanes):
    row = lax.broadcasted_iota(jnp.int32, (2 * lanes, lanes), 0)
    col = lax.broadcasted_iota(jnp.int32, (2 * lanes, lanes), 1)
    return jnp.where(row // 2 == col, 1.0, 0.0).astype(jnp.bfloat16)


def pooled_rows(fine_ref, matrix):
    fields, cells_y, _ = fine_ref.shape
    rows = cells_y // 4
    parts = [[fine_ref[f, pl.ds(k, rows, stride=4), :] for k in range(4)] for f in range(fields)]
    low = jnp.concatenate([p[0] + p[1] for p in parts], axis=0)
    high = jnp.concatenate([p[2] + p[3] for p in parts], axis=0)
    both = jnp.concatenate([low, high], axis=1)
    first = both.astype(jnp.bfloat16)
    rest = both - first.astype(jnp.float32)
    second = rest.astype(jnp.bfloat16)
    dot = functools.partial(jnp.dot, preferred_element_type=jnp.float32)
    return dot(first, matrix) + dot(second, matrix)


def tile_values(load, fields, span, tile_rows, lanes):
    sub = lax.broadcasted_iota(jnp.int32, (8, lanes), 0)
    values = []
    for v in range(tile_rows // 8):
        value = None
        for f in reversed(range(fields)):
            lo, hi = f * span - 8 * v, (f + 1) * span - 8 * v
            if hi <= 0 or lo >= 8:
                continue
            piece = load(f, -lo)
            value = piece if value is None else jnp.where(sub < hi, piece, value)
        values.append(value)
    return values


def send_tile(slot, at, values, stage, out, tile_rows, sem):
    for v, value in enumerate(values):
        stage[pl.ds(pl.multiple_of(at * tile_rows + 8 * v, 8), 8), :] = value
    here = pl.ds(pl.multiple_of(at * tile_rows, 8), tile_rows)
    there = pl.ds(pl.multiple_of(slot * tile_rows, 8), tile_rows)
    pltpu.make_async_copy(stage.at[here], out.at[there], sem).start()


def await_tiles(first, count, stage, out, tile_rows, sem):
    rows = count * tile_rows
    pltpu.make_async_copy(stage.at[pl.ds(first * tile_rows, rows)], out.at[pl.ds(0, rows)], sem).wait()


def edge_tiles(rows, span):
    return -(-rows // span)


def face_kernel(state, first, last, sems):
    cells_x = state.shape[1]
    one = pltpu.make_async_copy(state.at[:, 0], first, sems.at[0])
    two = pltpu.make_async_copy(state.at[:, cells_x - 1], last, sems.at[1])
    one.start()
    two.start()
    one.wait()
    two.wait()


def faces_of(state):
    fields, _, cells_y, lanes = state.shape
    face = jax.ShapeDtypeStruct((fields, cells_y, lanes), jnp.float32)
    vmem = pl.BlockSpec(memory_space=pltpu.VMEM)
    return pl.pallas_call(
        face_kernel,
        out_shape=(face, face),
        in_specs=[pl.BlockSpec(memory_space=pltpu.HBM)],
        out_specs=(vmem, vmem),
        scratch_shapes=[pltpu.SemaphoreType.DMA((2,))],
        compiler_params=pltpu.CompilerParams(vmem_limit_bytes=2 * MIB),
        cost_estimate=pl.CostEstimate(flops=0, bytes_accessed=650_000, transcendentals=0),
        name="faces",
    )(in_hbm(state))


def main_kernel(
    capacity, myself, coupling, target, state, adjoint, source, kappa, flags,
    out, slots, duals, sv, av, bv, kv, fv, wv, pv, tv, seen, sems, tsem,
):
    fields, cells_x, cells_y, lanes = adjoint.shape
    steps = cells_x // PLANES
    rows = cells_y // 4
    owners, per_dev = target.shape

    def copy(step, i):
        at = pl.ds(PLANES * step, PLANES)
        if i == 0:
            landing = sv.at[:, pl.ds(PLANES * step + 1, PLANES), pl.ds(8, cells_y)]
            return pltpu.make_async_copy(state.at[:, at], landing, sems.at[step, 0])
        if i > 2:
            src, dst = ((kappa, kv), (flags, fv))[i - 3]
            return pltpu.make_async_copy(src.at[at], dst.at[at], sems.at[step, i])
        src, dst = ((adjoint, av), (source, bv))[i - 1]
        return pltpu.make_async_copy(src.at[:, at], dst.at[:, at], sems.at[step, i])

    def start(step):
        copy(step + 1, 0).start()
        for i in range(1, 5):
            copy(step, i).start()

    me = myself[0]
    row8 = pl.multiple_of(lax.shift_left(lax.shift_right_logical(me, 3), 3), 8)
    table = pltpu.make_async_copy(target.at[pl.ds(row8, 8)], tv, tsem.at[0])
    table.start()
    copy(0, 0).start()
    for step in range(steps - 1):
        start(step)
    for i in range(1, 5):
        copy(steps - 1, i).start()
    zero = jnp.zeros((8, lanes), jnp.float32)
    pv[...] = pool_matrix(lanes)

    def clear(x, carry):
        for f in range(fields):
            sv[f, x, pl.ds(0, 8), :] = zero
            sv[f, x, pl.ds(cells_y + 8, 8), :] = zero
        return carry

    lax.fori_loop(0, cells_x + 2, clear, 0)
    for f in range(fields):
        for y in range(0, cells_y, 8):
            sv[f, 0, pl.ds(y + 8, 8), :] = zero
            sv[f, cells_x + 1, pl.ds(y + 8, 8), :] = zero

    for i in range(owners):
        seen[i] = 0
    table.wait()
    mine = lax.bitwise_and(me, 7)

    def rank(t, carry):
        owner = lax.shift_right_logical(tv[mine, t], per_dev.bit_length() - 1)
        count = seen[owner]
        slots[t] = owner * capacity + count
        seen[owner] = count + 1
        return carry

    lax.fori_loop(0, per_dev, rank, 0, unroll=8)

    coef = [[coupling[f, h] for h in range(fields)] for f in range(fields)]
    lane = lax.broadcasted_iota(jnp.int32, (8, lanes), 1)
    inner_lo = lane != 0
    inner_hi = lane != lanes - 1

    def pool(half, at):
        pooled = pooled_rows(wv.at[half], pv[...])
        for f in range(fields):
            out[f, pl.ds(pl.multiple_of(at + PAD, 8), rows), :] = pooled[f * rows : (f + 1) * rows]

    copy(0, 0).wait()
    def step_body(step, carry):
        @pl.when(step + 1 < steps)
        def _():
            copy(step + 1, 0).wait()

        for i in range(1, 5):
            copy(step, i).wait()

        for half in range(PLANES // 2):
            coarse = step * (PLANES // 2) + half
            pool(1 - half % 2, jnp.maximum(coarse - 1, 0) * rows)
            for y in range(0, cells_y, 8):
                total = [None] * fields
                for p in range(2):
                    x = 2 * coarse + p
                    kap = kv[x, pl.ds(y, 8), :]
                    wgt = weight_of(fv[x, pl.ds(y, 8), :])
                    mid = [sv[f, x + 1, pl.ds(y + 8, 8), :] for f in range(fields)]
                    for f in range(fields):
                        near = sv[f, x, pl.ds(y + 8, 8), :] + sv[f, x + 2, pl.ds(y + 8, 8), :]
                        near = near + sv[f, x + 1, pl.ds(y + 7, 8), :] + sv[f, x + 1, pl.ds(y + 9, 8), :]
                        near = near + jnp.where(inner_lo, pltpu.roll(mid[f], 1, 1), 0.0)
                        near = near + jnp.where(inner_hi, pltpu.roll(mid[f], lanes - 1, 1), 0.0)
                        applied = (kap + (coef[f][f] + 6.0)) * mid[f]
                        for h in range(fields):
                            if h != f:
                                applied = applied + coef[f][h] * mid[h]
                        residual = bv[f, x, pl.ds(y, 8), :] - applied + near
                        term = wgt * av[f, x, pl.ds(y, 8), :] * residual
                        total[f] = term if p == 0 else total[f] + term
                for f in range(fields):
                    wv[half % 2, f, pl.ds(y, 8), :] = total[f]
        return carry

    lax.fori_loop(0, steps, step_body, 0)
    pool(1, (cells_x // 2 - 1) * rows)
    for i, x in enumerate((0, cells_x - 1)):
        for y in range(0, cells_y, 8):
            wgt = weight_of(fv[x, pl.ds(y, 8), :])
            for f in range(fields):
                duals[i, f, pl.ds(y, 8), :] = wgt * av[f, x, pl.ds(y, 8), :]

def main_part(state, adjoint, source, kappa, flags, coupling, target, myself, capacity):
    fields, cells_x, cells_y, lanes = state.shape
    owners, per_dev = target.shape
    f32 = jnp.float32
    hbm = pl.BlockSpec(memory_space=pltpu.HBM)
    vmem = pl.BlockSpec(memory_space=pltpu.VMEM)
    smem = pl.BlockSpec(memory_space=pltpu.SMEM)
    return pl.pallas_call(
        functools.partial(main_kernel, capacity),
        out_shape=(
            jax.ShapeDtypeStruct((fields, cells_x * cells_y // 8 + 2 * PAD, lanes), f32),
            jax.ShapeDtypeStruct((per_dev,), jnp.int32),
            jax.ShapeDtypeStruct((2, fields, cells_y, lanes), f32),
        ),
        in_specs=[smem, smem, hbm, hbm, hbm, hbm, hbm, hbm],
        out_specs=(vmem, smem, vmem),
        scratch_shapes=[
            pltpu.VMEM((fields, cells_x + 2, cells_y + 16, lanes), f32),
            pltpu.VMEM((fields, cells_x, cells_y, lanes), f32),
            pltpu.VMEM((fields, cells_x, cells_y, lanes), f32),
            pltpu.VMEM((cells_x, cells_y, lanes), f32),
            pltpu.VMEM((cells_x, cells_y, lanes), jnp.int32),
            pltpu.VMEM((2, fields, cells_y, lanes), f32),
            pltpu.VMEM((2 * lanes, lanes), jnp.bfloat16),
            pltpu.SMEM((8, per_dev), jnp.int32),
            pltpu.SMEM((owners,), jnp.int32),
            pltpu.SemaphoreType.DMA((cells_x // PLANES, 5)),
            pltpu.SemaphoreType.DMA((1,)),
        ],
        compiler_params=pltpu.CompilerParams(vmem_limit_bytes=36 * MIB),
        cost_estimate=pl.CostEstimate(flops=100_000_000, bytes_accessed=27_700_000, transcendentals=0),
        name="residual_pool",
    )(myself, in_hbm(coupling), in_hbm(target), in_hbm(state), in_hbm(adjoint), in_hbm(source), in_hbm(kappa), in_hbm(flags))


def pack_kernel(tile_rows, odd, slots, part, duals, inner, outer, out, stage, pe, wv, pv, sem):
    fields, cells_y, lanes = inner.shape
    rows = cells_y // 4
    per_dev = slots.shape[0]
    cells = part.shape[1] - 2 * PAD
    span = cells // per_dev
    kept = pe.shape[2] - 2 * PAD
    edge = edge_tiles(rows, span)
    for t in range(edge, per_dev - edge):
        values = tile_values(
            lambda f, d: part[f, pl.ds(PAD + span * t + d, 8), :], fields, span, tile_rows, lanes
        )
        send_tile(slots[t], t, values, stage, out, tile_rows, sem.at[0])
    pv[...] = pool_matrix(lanes)
    swapped = odd[0] != 0
    for f in range(fields):
        for y in range(0, cells_y, 8):
            here = pl.ds(y, 8)
            near, far = inner[f, here, :], outer[f, here, :]
            wv[0, f, here, :] = duals[0, f, here, :] * jnp.where(swapped, near, far)
            wv[1, f, here, :] = duals[1, f, here, :] * jnp.where(swapped, far, near)
    pooled = [pooled_rows(wv.at[i], pv[...]) for i in range(2)]
    for i, (at, start) in enumerate(((0, 0), (kept - rows, cells - kept))):
        for f in range(fields):
            pe[i, f, pl.ds(PAD, kept), :] = part[f, pl.ds(PAD + start, kept), :]
            here = pl.ds(at + PAD, rows)
            pe[i, f, here, :] = pe[i, f, here, :] + pooled[i][f * rows : (f + 1) * rows]
    for i, (tile, start) in enumerate(((0, 0), (per_dev - edge, kept - edge * span))):
        for k in range(edge):
            values = tile_values(
                lambda f, d: pe[i, f, pl.ds(PAD + start + span * k + d, 8), :], fields, span, tile_rows, lanes
            )
            send_tile(slots[tile + k], tile + k, values, stage, out, tile_rows, sem.at[0])
    await_tiles(0, per_dev, stage, out, tile_rows, sem.at[0])


def pack_part(odd, part, slots, duals, inner, outer, n_slots, tile_rows):
    fields, cells_y, lanes = inner.shape
    per_dev = slots.shape[0]
    span = (part.shape[1] - 2 * PAD) // per_dev
    kept = -(-edge_tiles(cells_y // 4, span) * span // 8) * 8
    f32 = jnp.float32
    vmem = pl.BlockSpec(memory_space=pltpu.VMEM)
    return pl.pallas_call(
        functools.partial(pack_kernel, tile_rows),
        out_shape=pltpu.HBM((n_slots * tile_rows, lanes), f32),
        in_specs=[pl.BlockSpec(memory_space=pltpu.SMEM)] * 2 + [vmem] * 4,
        out_specs=pl.BlockSpec(memory_space=pltpu.HBM),
        scratch_shapes=[
            pltpu.VMEM((per_dev * tile_rows, lanes), f32),
            pltpu.VMEM((2, fields, kept + 2 * PAD, lanes), f32),
            pltpu.VMEM((2, fields, cells_y, lanes), f32),
            pltpu.VMEM((2 * lanes, lanes), jnp.bfloat16),
            pltpu.SemaphoreType.DMA((1,)),
        ],
        compiler_params=pltpu.CompilerParams(vmem_limit_bytes=12 * MIB),
        cost_estimate=pl.CostEstimate(flops=1_000_000, bytes_accessed=3_500_000, transcendentals=0),
        name="edges_pack",
    )(odd, slots, part, duals, inner, outer)


def unpack_kernel(tile_rows, lookup, received, out, stage, built, sems):
    fields, per_dev, width = built.shape
    lanes = received.shape[1]
    span = width // lanes
    piece = per_dev // sems.shape[0]

    def leave(k):
        here = pl.ds(k * piece, piece)
        return pltpu.make_async_copy(built.at[:, here], out.at[:, here], sems.at[k])

    for g in range(per_dev // 8):
        buf = stage.at[g % stage.shape[0]]
        for s in range(8):
            base = pl.multiple_of(lookup[g * 8 + s] * tile_rows, 8)
            buf[pl.ds(s * (tile_rows + 1), tile_rows), :] = received[pl.ds(base, tile_rows), :]
        for f in range(fields):
            for j in range(span):
                rows = buf[pl.ds(f * span + j, 8, stride=tile_rows + 1), :]
                built[f, pl.ds(g * 8, 8), pl.ds(j * lanes, lanes)] = rows
        if (g + 1) * 8 % piece == 0:
            leave(g * 8 // piece).start()
    for k in range(sems.shape[0]):
        leave(k).wait()


def unpack_part(lookup, received, fields, per_dev, width, tile_rows):
    lanes = received.shape[1]
    return pl.pallas_call(
        functools.partial(unpack_kernel, tile_rows),
        out_shape=jax.ShapeDtypeStruct((fields, per_dev, width), jnp.float32),
        in_specs=[pl.BlockSpec(memory_space=pltpu.SMEM), pl.BlockSpec(memory_space=pltpu.VMEM)],
        out_specs=pl.BlockSpec(memory_space=pltpu.HBM),
        scratch_shapes=[
            pltpu.VMEM((per_dev // 8, 8 * (tile_rows + 1), lanes), jnp.float32),
            pltpu.VMEM((fields, per_dev, width), jnp.float32),
            pltpu.SemaphoreType.DMA((4,)),
        ],
        compiler_params=pltpu.CompilerParams(vmem_limit_bytes=8 * MIB),
        cost_estimate=pl.CostEstimate(flops=0, bytes_accessed=3_000_000, transcendentals=0),
        name="unpack",
    )(lookup, received)


def local(state, adjoint, source, kappa, cut_flags, coupling, target):
    state, adjoint, source, kappa, flags = (a[0] for a in (state, adjoint, source, kappa, cut_flags))
    fields, cells_x, cells_y, lanes = state.shape
    groups, bricks = lax.axis_size("grp"), lax.axis_size("brk")
    owners = groups * bricks
    per_dev = target.shape[1]
    capacity = per_dev // ((groups - 1) * bricks) + 1
    width = cells_x * cells_y * lanes // 8 // per_dev
    span = width // lanes
    tile_rows = -(-span * fields // 8) * 8
    myself = lax.axis_index(("grp", "brk"))

    odd = lax.rem(lax.axis_index("brk"), 2)
    one = [(i, i ^ 1) for i in range(bricks)]
    two = [(i, j) for i in range(1, bricks - 1) for j in (((i - 1) ^ 1) + 1,)]
    planes = state.reshape(fields * cells_x, cells_y, lanes)
    first = lax.slice(planes, (0, 0, 0), planes.shape, (cells_x, 1, 1))
    last = lax.slice(planes, (cells_x - 1, 0, 0), planes.shape, (cells_x, 1, 1))
    inner = lax.ppermute(jnp.where(odd == 0, last, first), "brk", one)
    outer = lax.ppermute(jnp.where(odd == 0, first, last), "brk", two)

    part, slots, duals = main_part(
        state, adjoint, source, kappa, flags, coupling, target, myself.reshape(1), capacity
    )
    outgoing = pack_part(odd.reshape(1), part, slots, duals, inner, outer, owners * capacity, tile_rows)
    outgoing = outgoing.reshape(owners, capacity * tile_rows, lanes)
    incoming = lax.all_to_all(outgoing, ("grp", "brk"), 0, 0, tiled=True)
    incoming = incoming.reshape(owners * capacity * tile_rows, lanes)

    slot_ids = myself * per_dev + jnp.arange(per_dev, dtype=jnp.int32)
    codes = jnp.arange(owners * per_dev, dtype=jnp.int32)
    hit = target.reshape(-1)[None, :] == slot_ids[:, None]
    origin = jnp.sum(jnp.where(hit, codes[None, :], 0), axis=1)
    sender = origin // per_dev
    before_it = jnp.logical_and(sender[:, None] == sender[None, :], origin[None, :] < origin[:, None])
    lookup = sender * capacity + jnp.sum(before_it.astype(jnp.int32), axis=1)
    out = unpack_part(lookup, incoming, fields, per_dev, width, tile_rows)
    return out.transpose(1, 0, 2)


def solution(mesh):
    placed = (
        P("grp", None, "brk", None, None),
        P("grp", None, "brk", None, None),
        P("grp", None, "brk", None, None),
        P("grp", "brk", None, None),
        P("grp", "brk", None, None),
        P(),
        P(),
    )
    return jax.shard_map(
        local, mesh=mesh, in_specs=placed, out_specs=P(("grp", "brk"), None, None), check_vma=False
    )
```
